32 devices in a mesh: dp: 8 (over z, x), seq: 4 (over y, core).
Axes of the slice: x: 2, y: 2, z: 4, core: 2. Of those that a mesh axis runs over, the one named last changes fastest.
Arguments:
- tokens: float32 [16, 256, 1024], P('dp', 'seq'), may hold values from -6 to 6
- output_cotangent: float32 [16, 256, 1024], P('dp', 'seq'), may hold values from -0.5 to 0.5
- placement: int32 [8], replicated, may hold values from 0 to 15, as said below
- inward: float32 [1024, 3072], P(('dp', 'seq'))
- outward: float32 [1024, 1024], P(('dp', 'seq')), may hold values from -0.75 to 0.75
- attend_vectors: float32 [5, 1024], P(None, ('dp', 'seq'))
- expand: float32 [1024, 4096], P(('dp', 'seq')), may hold values from -0.1875 to 0.1875
- shrink: float32 [4096, 1024], P(('dp', 'seq')), may hold values from -0.09375 to 0.09375
- feed_vectors: float32 [3, 1024], P(None, ('dp', 'seq'))
- expand_bias: float32 [4096], P(('dp', 'seq')), may hold values from -3 to 3
- inward_moments: float32 [2, 1024, 3072], P(None, ('dp', 'seq')), as said below
- outward_moments: float32 [2, 1024, 1024], P(None, ('dp', 'seq'))
- attend_moments: float32 [2, 5, 1024], P(None, None, ('dp', 'seq'))
- expand_moments: float32 [2, 1024, 4096], P(None, ('dp', 'seq'))
- shrink_moments: float32 [2, 4096, 1024], P(None, ('dp', 'seq'))
- feed_moments: float32 [2, 3, 1024], P(None, None, ('dp', 'seq'))
- bias_moments: float32 [2, 4096], P(None, ('dp', 'seq'))
Outputs:
- block_output: float32 [16, 256, 1024], P('dp', 'seq')
- input_gradient: float32 [16, 256, 1024], P('dp', 'seq')
- inward_gradient: float32 [1024, 3072], P(('dp', 'seq'))
- outward_gradient: float32 [1024, 1024], P(('dp', 'seq'))
- attend_gradient: float32 [5, 1024], P(None, ('dp', 'seq'))
- expand_gradient: float32 [1024, 4096], P(('dp', 'seq'))
- shrink_gradient: float32 [4096, 1024], P(('dp', 'seq'))
- feed_gradient: float32 [3, 1024], P(None, ('dp', 'seq'))
- bias_gradient: float32 [4096], P(('dp', 'seq'))
- inward_new: float32 [1024, 3072], P(('dp', 'seq'))
- outward_new: float32 [1024, 1024], P(('dp', 'seq'))
- attend_new: float32 [5, 1024], P(None, ('dp', 'seq'))
- expand_new: float32 [1024, 4096], P(('dp', 'seq'))
- shrink_new: float32 [4096, 1024], P(('dp', 'seq'))
- feed_new: float32 [3, 1024], P(None, ('dp', 'seq'))
- bias_new: float32 [4096], P(('dp', 'seq'))
- inward_state: float32 [2, 1024, 3072], P(None, ('dp', 'seq'))
- outward_state: float32 [2, 1024, 1024], P(None, ('dp', 'seq'))
- attend_state: float32 [2, 5, 1024], P(None, None, ('dp', 'seq'))
- expand_state: float32 [2, 1024, 4096], P(None, ('dp', 'seq'))
- shrink_state: float32 [2, 4096, 1024], P(None, ('dp', 'seq'))
- feed_state: float32 [2, 3, 1024], P(None, None, ('dp', 'seq'))
- bias_state: float32 [2, 4096], P(None, ('dp', 'seq'))
The draws below stay inside these ranges and needn't reach their ends.
Inputs may be any that keep to these rules, and one draw needn't show every extreme that they name: `placement`: entries are distinct slot numbers; slot s belongs to index s // 2 of dp; in every draw some index of dp holds 2 sequences. `inward_moments`: the second moment (index 1) is positive.
All inputs are finite; a program needn't handle non-finite values.
Results may differ from the reference program's by a relative error of at most 0.012.
Values may be sent and summed in bfloat16 or wider, within the bound.
A program may use at most 192 MiB of HBM per device.

```python
import math
import jax
import jax.numpy as jnp
from jax import lax

D = 1024
HEADS = 16
HEAD_DIM = 64
FF = 4096
LEN = 256
SLOTS = 2
SLOTS_ALL = 16
NSEQ = 8


def moments_draw(key, shape):
    first_moment = 2.0 * jax.random.normal(jax.random.fold_in(key, 11), shape, jnp.float32)
    second = jnp.exp(jax.random.uniform(jax.random.fold_in(key, 12), shape, jnp.float32, -1.386, 1.386))
    return jnp.stack([first_moment, second])


def vectors_draw(key, count):
    gains = 1.0 + 0.2 * jax.random.normal(jax.random.fold_in(key, 21), (1, D), jnp.float32)
    others = 0.5 * jax.random.normal(jax.random.fold_in(key, 22), (count - 1, D), jnp.float32)
    return jnp.concatenate([gains, others], axis=0)


def draw_placement(key, part):
    shuffled = jax.random.permutation(jax.random.fold_in(key, 3), SLOTS_ALL)
    ranking = jnp.zeros((SLOTS_ALL,), jnp.int32).at[shuffled].set(jnp.arange(SLOTS_ALL, dtype=jnp.int32))
    chosen = jax.random.randint(jax.random.fold_in(key, 4), (), 0, SLOTS_ALL // SLOTS)
    slot_ids = jnp.arange(SLOTS_ALL, dtype=jnp.int32)
    priority = jnp.where(slot_ids // SLOTS == chosen, slot_ids % SLOTS - SLOTS, ranking)
    return jnp.argsort(priority)[:NSEQ].astype(jnp.int32)


def draw_inward(key, part):
    base = jax.random.normal(jax.random.fold_in(key, 1), (D, 3 * D), jnp.float32) * D ** (-0.5)
    return base


def draw_attend_vectors(key, part):
    return vectors_draw(key, 5)


def draw_feed_vectors(key, part):
    return vectors_draw(key, 3)


def draw_inward_moments(key, part):
    return moments_draw(key, (D, 3 * D))


def draw_outward_moments(key, part):
    return moments_draw(key, (D, D))


def draw_attend_moments(key, part):
    return moments_draw(key, (5, D))


def draw_expand_moments(key, part):
    return moments_draw(key, (D, FF))


def draw_shrink_moments(key, part):
    return moments_draw(key, (FF, D))


def draw_feed_moments(key, part):
    return moments_draw(key, (3, D))


def draw_bias_moments(key, part):
    return moments_draw(key, (FF,))


def shard_levels(own_key, dims, shards, low, largest):
    def one(dim, parts):
        steps = jax.random.uniform(jax.random.fold_in(jax.random.fold_in(own_key, 6), dim), (parts,), jnp.float32, low / len(shards), largest / len(shards))
        return jnp.repeat(jnp.exp(steps), dims[dim] // parts).reshape((-1,) + (1,) * (len(dims) - dim - 1))

    loudness = one(*shards[0])
    for cut in shards[1:]:
        loudness = loudness * one(*cut)
    return loudness


def scatter_about(stream_key, dims, deviation, limit, pieces=(), kind=jnp.bfloat16):
    array = jax.random.normal(stream_key, dims, jnp.float32) * deviation
    if len(pieces) > 0:
        array = shard_levels(stream_key, dims, pieces, -0.22, 0.18) * array
    return jnp.clip(array, min=-limit, max=limit).astype(kind)


def setup_inputs(seed: int = 0) -> dict:
    splits = jax.random.split(jax.random.key(seed), 18)
    tokens = scatter_about(splits[0], (SLOTS_ALL, LEN, D), 1.0, 6.0, ((0, 8), (1, 4)), jnp.float32)
    output_cotangent = scatter_about(splits[1], (SLOTS_ALL, LEN, D), (4.0 / (NSEQ * LEN) ** 0.5), 0.5, ((0, 8), (1, 4)), jnp.float32)
    placement = draw_placement(jax.random.fold_in(splits[17], 71), 0)
    inward = draw_inward(jax.random.fold_in(splits[17], 71), 0)
    outward = scatter_about(splits[4], (D, D), (D // 16) ** -0.5, 0.75, ((0, 32),), jnp.float32)
    attend_vectors = draw_attend_vectors(jax.random.fold_in(splits[17], 71), 0)
    expand = scatter_about(splits[6], (D, FF), D ** -0.5, 0.1875, ((0, 32),), jnp.float32)
    shrink = scatter_about(splits[7], (FF, D), FF ** -0.5, 0.09375, ((0, 32),), jnp.float32)
    feed_vectors = draw_feed_vectors(jax.random.fold_in(splits[17], 71), 0)
    expand_bias = scatter_about(splits[9], (FF,), 0.5, 3.0, ((0, 32),), jnp.float32)
    inward_moments = draw_inward_moments(jax.random.fold_in(splits[17], 71), 0)
    outward_moments = draw_outward_moments(jax.random.fold_in(splits[17], 71), 0)
    attend_moments = draw_attend_moments(jax.random.fold_in(splits[17], 71), 0)
    expand_moments = draw_expand_moments(jax.random.fold_in(splits[17], 71), 0)
    shrink_moments = draw_shrink_moments(jax.random.fold_in(splits[17], 71), 0)
    feed_moments = draw_feed_moments(jax.random.fold_in(splits[17], 71), 0)
    bias_moments = draw_bias_moments(jax.random.fold_in(splits[17], 71), 0)
    return {"tokens": tokens, "output_cotangent": output_cotangent, "placement": placement, "inward": inward, "outward": outward, "attend_vectors": attend_vectors, "expand": expand, "shrink": shrink, "feed_vectors": feed_vectors, "expand_bias": expand_bias, "inward_moments": inward_moments, "outward_moments": outward_moments, "attend_moments": attend_moments, "expand_moments": expand_moments, "shrink_moments": shrink_moments, "feed_moments": feed_moments, "bias_moments": bias_moments}


norm_epsilon = 1e-05
beta_first = 0.9
beta_second = 0.95
adam_epsilon = 1e-08
learn_rate = 0.01
weight_decay = 0.1
adam_steps = 4
gelu_scale = 0.7978845608028654
gelu_cubic = 0.044715
masked_score = -1e+30

def halved(operand):
    return operand.astype(jnp.bfloat16)

def normalize(operand):
    average = lax.optimization_barrier(jnp.mean(operand, axis=-1, keepdims=True))
    centered = operand - average
    variance = lax.optimization_barrier(jnp.mean(centered * centered, axis=-1, keepdims=True))
    inverse = lax.rsqrt(variance + norm_epsilon)
    return (centered * inverse, inverse)

def norm_back(upstream, normed, inverse):
    first_mean = lax.optimization_barrier(jnp.mean(upstream, axis=-1, keepdims=True))
    second_mean = lax.optimization_barrier(jnp.mean(upstream * normed, axis=-1, keepdims=True))
    return inverse * (upstream - first_mean - normed * second_mean)

def gelu_pair(upper):
    inner_arg = gelu_scale * (upper + gelu_cubic * upper * upper * upper)
    tangent = jnp.tanh(inner_arg)
    active = 0.5 * upper * (1.0 + tangent)
    slope = 0.5 * (1.0 + tangent) + 0.5 * upper * (1.0 - tangent * tangent) * gelu_scale * (1.0 + 3.0 * gelu_cubic * upper * upper)
    return (active, slope)

def adamw_update(parameter, gradient, moments, decay_rate):
    first_moment = beta_first * moments[0] + (1.0 - beta_first) * gradient
    second = beta_second * moments[1] + (1.0 - beta_second) * gradient * gradient
    unbiased_first = first_moment / (1.0 - beta_first ** adam_steps)
    unbiased_second = second / (1.0 - beta_second ** adam_steps)
    update = unbiased_first / (jnp.sqrt(unbiased_second) + adam_epsilon) + decay_rate * parameter
    return (parameter - learn_rate * update, jnp.stack([first_moment, second]))

def forward_backward(weights, tokens, cotangent):
    proj_in, proj_out, vectors_one, proj_up, proj_down, vectors_two, bias_up = weights
    highest = lax.Precision.HIGHEST
    length = tokens.shape[0]
    model_width = tokens.shape[1]
    score_scale = 1.0 / math.sqrt(HEAD_DIM)
    vec_one = vectors_one.astype(jnp.float32)
    vec_two = vectors_two.astype(jnp.float32)
    normed_one, inverse_one = normalize(tokens)
    lifted_one = halved(normed_one * vec_one[0] + vec_one[1])
    packed = jnp.dot(lifted_one, proj_in, preferred_element_type=jnp.float32)
    queries = halved(packed[:, :model_width] + vec_one[2])
    key_half = halved(packed[:, model_width:2 * model_width])
    value_half = halved(packed[:, 2 * model_width:] + vec_one[3])
    query_heads = queries.astype(jnp.float32).reshape(length, HEADS, HEAD_DIM)
    key_heads = key_half.astype(jnp.float32).reshape(length, HEADS, HEAD_DIM)
    value_heads = value_half.astype(jnp.float32).reshape(length, HEADS, HEAD_DIM)
    positions = jnp.arange(length)
    allowed = positions[None, :] <= positions[:, None]
    scores = jnp.einsum('qhd,khd->hqk', query_heads, key_heads, precision=highest) * score_scale
    scores = jnp.where(allowed[None], scores, masked_score)
    score_peak = lax.optimization_barrier(jnp.max(scores, axis=-1, keepdims=True))
    log_total = score_peak + jnp.log(lax.optimization_barrier(jnp.sum(jnp.exp(scores - score_peak), axis=-1, keepdims=True)))
    weights_full = jnp.exp(scores - log_total)
    weights_half = halved(weights_full)
    attended = halved(jnp.einsum('hqk,khd->qhd', weights_half.astype(jnp.float32), value_heads, precision=highest).reshape(length, model_width))
    middle = tokens + jnp.dot(attended, proj_out, preferred_element_type=jnp.float32) + vec_one[4]
    normed_two, inverse_two = normalize(middle)
    lifted_two = halved(normed_two * vec_two[0] + vec_two[1])
    upper_act = jnp.dot(lifted_two, proj_up, preferred_element_type=jnp.float32) + bias_up.astype(jnp.float32)
    active_full, gelu_slope = gelu_pair(upper_act)
    active = halved(active_full)
    block_out = middle + jnp.dot(active, proj_down, preferred_element_type=jnp.float32) + vec_two[2]
    cot_half = halved(cotangent)
    shrink_grad = jnp.dot(active.T, cot_half, preferred_element_type=jnp.float32)
    feed_bias_grad = lax.optimization_barrier(jnp.sum(cotangent, axis=0))
    upper_grad = jnp.dot(cot_half, proj_down.T, preferred_element_type=jnp.float32) * gelu_slope
    upper_half = halved(upper_grad)
    expand_grad = jnp.dot(lifted_two.T, upper_half, preferred_element_type=jnp.float32)
    expand_bias_grad = lax.optimization_barrier(jnp.sum(upper_grad, axis=0))
    lift_two_grad = jnp.dot(upper_half, proj_up.T, preferred_element_type=jnp.float32)
    gain_two_grad = lax.optimization_barrier(jnp.sum(lift_two_grad * normed_two, axis=0))
    shift_two_grad = lax.optimization_barrier(jnp.sum(lift_two_grad, axis=0))
    middle_grad = cotangent + norm_back(lift_two_grad * vec_two[0], normed_two, inverse_two)
    middle_half = halved(middle_grad)
    outward_grad = jnp.dot(attended.T, middle_half, preferred_element_type=jnp.float32)
    out_bias_grad = lax.optimization_barrier(jnp.sum(middle_grad, axis=0))
    attended_grad = halved(jnp.dot(middle_half, proj_out.T, preferred_element_type=jnp.float32))
    grad_heads = attended_grad.astype(jnp.float32).reshape(length, HEADS, HEAD_DIM)
    attended_heads = attended.astype(jnp.float32).reshape(length, HEADS, HEAD_DIM)
    delta_sum = lax.optimization_barrier(jnp.sum(grad_heads * attended_heads, axis=-1))
    weight_grad = jnp.einsum('qhd,khd->hqk', grad_heads, value_heads, precision=highest)
    score_grad = halved(weights_full * (weight_grad - delta_sum.T[:, :, None]) * score_scale).astype(jnp.float32)
    query_grad = jnp.einsum('hqk,khd->qhd', score_grad, key_heads, precision=highest).reshape(length, model_width)
    key_grad = jnp.einsum('hqk,qhd->khd', score_grad, query_heads, precision=highest).reshape(length, model_width)
    value_grad = jnp.einsum('hqk,qhd->khd', weights_half.astype(jnp.float32), grad_heads, precision=highest).reshape(length, model_width)
    packed_grad = halved(jnp.concatenate([query_grad, key_grad, value_grad], axis=1))
    inward_grad = jnp.dot(lifted_one.T, packed_grad, preferred_element_type=jnp.float32)
    query_bias_grad = lax.optimization_barrier(jnp.sum(query_grad, axis=0))
    value_bias_grad = lax.optimization_barrier(jnp.sum(value_grad, axis=0))
    lift_one_grad = jnp.dot(packed_grad, proj_in.T, preferred_element_type=jnp.float32)
    gain_one_grad = lax.optimization_barrier(jnp.sum(lift_one_grad * normed_one, axis=0))
    shift_one_grad = lax.optimization_barrier(jnp.sum(lift_one_grad, axis=0))
    tokens_grad = middle_grad + norm_back(lift_one_grad * vec_one[0], normed_one, inverse_one)
    gradients = (inward_grad, outward_grad, jnp.stack([gain_one_grad, shift_one_grad, query_bias_grad, value_bias_grad, out_bias_grad]), expand_grad, shrink_grad, jnp.stack([gain_two_grad, shift_two_grad, feed_bias_grad]), expand_bias_grad)
    return (block_out, tokens_grad, gradients)

def reference(tokens, output_cotangent, placement, inward, outward, attend_vectors, expand, shrink, feed_vectors, expand_bias, inward_moments, outward_moments, attend_moments, expand_moments, shrink_moments, feed_moments, bias_moments):
    masters = (inward, outward, attend_vectors, expand, shrink, feed_vectors, expand_bias)
    rounded = tuple((halved(member) for member in masters))
    live_tokens = tokens[placement]
    live_cot = output_cotangent[placement]
    zero_grads = tuple((jnp.zeros(member.shape, jnp.float32) for member in masters))

    def visit(totals, inputs_pair):
        block_out, tokens_grad, gradients = forward_backward(rounded, inputs_pair[0], inputs_pair[1])
        summed = tuple((left + right for left, right in zip(totals, gradients)))
        return (summed, (block_out, tokens_grad))
    totals, (outputs, input_grads) = lax.scan(visit, zero_grads, (live_tokens, live_cot))
    block_output = jnp.zeros(tokens.shape, jnp.float32).at[placement].set(outputs)
    input_gradient = jnp.zeros(tokens.shape, jnp.float32).at[placement].set(input_grads)
    moments_all = (inward_moments, outward_moments, attend_moments, expand_moments, shrink_moments, feed_moments, bias_moments)
    decays = (weight_decay, weight_decay, 0.0, weight_decay, weight_decay, 0.0, 0.0)
    fresh = []
    states = []
    for index_item in range(7):
        new_param, new_state = adamw_update(masters[index_item], totals[index_item], moments_all[index_item], decays[index_item])
        fresh.append(new_param)
        states.append(new_state)
    return (block_output, input_gradient, totals[0], totals[1], totals[2], totals[3], totals[4], totals[5], totals[6], fresh[0], fresh[1], fresh[2], fresh[3], fresh[4], fresh[5], fresh[6], states[0], states[1], states[2], states[3], states[4], states[5], states[6])
```

```python
import functools
import math
import types

import jax
import jax.numpy as jnp
from jax import lax
from jax.experimental import pallas as pl
from jax.experimental.pallas import tpu as pltpu
from jax.sharding import PartitionSpec as P

HEADS = 16
HEAD_DIM = 64


norm_epsilon = 1e-05
beta_first = 0.9
beta_second = 0.95
adam_epsilon = 1e-08
learn_rate = 0.01
weight_decay = 0.1
adam_steps = 4
gelu_scale = 0.7978845608028654
gelu_cubic = 0.044715
masked_score = -1e30


def halved(operand):
    return operand.astype(jnp.bfloat16)


def normalize(operand):
    average = jnp.mean(operand, axis=-1, keepdims=True)
    centered = operand - average
    variance = jnp.mean(centered * centered, axis=-1, keepdims=True)
    inverse = lax.rsqrt(variance + norm_epsilon)
    return (centered * inverse, inverse)


def norm_back(upstream, normed, inverse):
    first_mean = jnp.mean(upstream, axis=-1, keepdims=True)
    second_mean = jnp.mean(upstream * normed, axis=-1, keepdims=True)
    return inverse * (upstream - first_mean - normed * second_mean)


def gelu_pair(upper):
    inner_arg = gelu_scale * (upper + gelu_cubic * upper * upper * upper)
    tangent = jnp.tanh(inner_arg)
    active = 0.5 * upper * (1.0 + tangent)
    slope = 0.5 * (1.0 + tangent) + 0.5 * upper * (1.0 - tangent * tangent) * gelu_scale * (
        1.0 + 3.0 * gelu_cubic * upper * upper
    )
    return (active, slope)


def adamw_update(parameter, gradient, moments, decay_rate):
    first_moment = beta_first * moments[0] + (1.0 - beta_first) * gradient
    second = beta_second * moments[1] + (1.0 - beta_second) * gradient * gradient
    unbiased_first = first_moment / (1.0 - beta_first**adam_steps)
    unbiased_second = second / (1.0 - beta_second**adam_steps)
    update = unbiased_first / (jnp.sqrt(unbiased_second) + adam_epsilon) + decay_rate * parameter
    return (parameter - learn_rate * update, jnp.stack([first_moment, second]))


def collect_columns(piece, groups, inner):
    rows = piece.shape[0] // groups
    parts = piece.reshape(rows * groups, -1, 1, inner)
    moved = lax.all_to_all(parts, "seq", 0, 2, tiled=True)
    return moved.reshape(rows, -1)


def body(
    tokens,
    output_cotangent,
    placement,
    inward,
    outward,
    attend_vectors,
    expand,
    shrink,
    feed_vectors,
    expand_bias,
    inward_moments,
    outward_moments,
    attend_moments,
    expand_moments,
    shrink_moments,
    feed_moments,
    bias_moments,
):
    slot_count, block_size, model_width = tokens.shape
    groups = lax.axis_size("seq")
    replicas = lax.axis_size("dp")
    devices = groups * replicas
    mine = lax.axis_index("seq")
    length = block_size * groups
    row_count = slot_count * block_size
    all_rows = slot_count * length
    head_count = HEADS // groups
    part_width = head_count * HEAD_DIM
    vec_width = attend_vectors.shape[1]
    hidden_part = expand_bias.shape[0]
    score_scale = 1.0 / math.sqrt(HEAD_DIM)

    def gather_rows(local):
        full = lax.all_gather(
            local.reshape(slot_count, block_size, -1), "seq", axis=1, tiled=True
        )
        return full.reshape(all_rows, -1)

    def scatter_rows(partial):
        own = lax.psum_scatter(
            halved(partial).reshape(slot_count, length, -1), "seq", scatter_dimension=1, tiled=True
        )
        return own.reshape(row_count, -1).astype(jnp.float32)

    slot_ids = lax.axis_index("dp") * slot_count + jnp.arange(slot_count, dtype=jnp.int32)
    live_mask = jnp.any(placement[None, :] == slot_ids[:, None], axis=1).astype(jnp.float32)[
        :, None, None
    ]

    small = jnp.concatenate(
        [
            halved(attend_vectors).reshape(-1),
            halved(feed_vectors).reshape(-1),
            halved(expand_bias),
        ]
    )
    small_size = small.shape[0]
    pad_rows = 16
    in_rows = inward.shape[0]
    block_rows = groups * in_rows
    small_row = jnp.broadcast_to(
        jnp.pad(small, (0, model_width - small_size)), (groups, 1, model_width)
    )
    both = jnp.concatenate([halved(inward), halved(outward)], axis=1)
    both_parts = jnp.transpose(both.reshape(in_rows, -1, groups, part_width), (2, 0, 1, 3))
    up_parts = jnp.transpose(
        halved(expand).reshape(in_rows, replicas, groups, hidden_part), (2, 0, 1, 3)
    )
    moved = lax.all_to_all(
        jnp.concatenate(
            [
                both_parts.reshape(groups, in_rows, model_width),
                up_parts.reshape(groups, in_rows, model_width),
                small_row,
            ],
            axis=1,
        ),
        "seq",
        0,
        0,
        tiled=True,
    )
    small_block = jnp.pad(moved[:, 2 * in_rows], ((0, pad_rows - groups), (0, 0)))
    first = lax.all_gather(
        jnp.concatenate(
            [moved[:, :in_rows].reshape(block_rows, model_width), small_block], axis=0
        ),
        "dp",
        axis=0,
        tiled=True,
    ).reshape(replicas, block_rows + pad_rows, model_width)
    both_part = first[:, :block_rows].reshape(model_width, model_width)
    in_part = both_part[:, : 3 * part_width]
    out_part = both_part[:, 3 * part_width :]
    small_all = (
        first[:, block_rows : block_rows + groups, :small_size]
        .reshape(devices, small_size)
        .astype(jnp.float32)
    )
    vectors = jnp.transpose(
        small_all[:, : 8 * vec_width].reshape(devices, 8, vec_width), (1, 0, 2)
    ).reshape(8, model_width)
    vec_one = vectors[:5]
    vec_two = vectors[5:]
    bias_all = small_all[:, 8 * vec_width :].reshape(replicas, groups, hidden_part)
    bias_part = lax.dynamic_index_in_dim(bias_all, mine, 1, keepdims=False).reshape(-1)
    up_part = lax.all_gather(
        moved[:, in_rows : 2 * in_rows].reshape(block_rows, model_width),
        "dp",
        axis=0,
        tiled=True,
    )
    down_part = lax.all_gather(halved(shrink), "dp", axis=0, tiled=True)

    cotangent = (output_cotangent * live_mask).reshape(row_count, model_width)
    cot_all = gather_rows(halved(cotangent))
    feed_bias_grad = jnp.sum(cotangent, axis=0)

    flat_tokens = tokens.reshape(row_count, model_width)
    normed_one, inverse_one = normalize(flat_tokens)
    lifted_one = gather_rows(halved(normed_one * vec_one[0] + vec_one[1]))
    packed = jnp.dot(lifted_one, in_part, preferred_element_type=jnp.float32)
    bias_query = lax.dynamic_slice_in_dim(vec_one[2], mine * part_width, part_width)
    bias_value = lax.dynamic_slice_in_dim(vec_one[3], mine * part_width, part_width)

    def to_heads(operand):
        return jnp.transpose(
            operand.reshape(slot_count, length, head_count, HEAD_DIM), (0, 2, 1, 3)
        )

    def from_heads(operand):
        return jnp.transpose(operand, (0, 2, 1, 3)).reshape(all_rows, part_width)

    queries = to_heads(halved(packed[:, :part_width] + bias_query))
    keys = to_heads(halved(packed[:, part_width : 2 * part_width]))
    values = to_heads(halved(packed[:, 2 * part_width :] + bias_value))
    positions = jnp.arange(length)
    allowed = positions[None, :] <= positions[:, None]
    scores = (
        jnp.einsum("shqd,shkd->shqk", queries, keys, preferred_element_type=jnp.float32)
        * score_scale
    )
    scores = jnp.where(allowed, scores, masked_score)
    score_peak = jnp.max(scores, axis=-1, keepdims=True)
    log_total = score_peak + jnp.log(jnp.sum(jnp.exp(scores - score_peak), axis=-1, keepdims=True))
    weights_full = jnp.exp(scores - log_total)
    weights_half = halved(weights_full)
    attended_heads = halved(
        jnp.einsum("shqk,shkd->shqd", weights_half, values, preferred_element_type=jnp.float32)
    )
    attended = lax.all_gather(from_heads(attended_heads), "seq", axis=0, tiled=False)
    attended = jnp.transpose(attended, (1, 0, 2)).reshape(all_rows, model_width)
    projected = lax.all_to_all(
        halved(jnp.dot(attended, out_part, preferred_element_type=jnp.float32)).reshape(
            slot_count, length, part_width
        ),
        "seq",
        1,
        2,
        tiled=True,
    ).reshape(row_count, model_width)
    middle = flat_tokens + projected + vec_one[4]
    normed_two, inverse_two = normalize(middle)
    lifted_two = gather_rows(halved(normed_two * vec_two[0] + vec_two[1]))
    upper = jnp.dot(lifted_two, up_part, preferred_element_type=jnp.float32) + bias_part
    active_full, slope = gelu_pair(upper)
    active = halved(active_full)
    upper_grad = (
        lax.dot_general(
            cot_all, down_part, (((1,), (1,)), ((), ())), preferred_element_type=jnp.float32
        )
        * slope
    )
    upper_half = halved(upper_grad)
    lift_two_grad = scatter_rows(
        lax.dot_general(
            upper_half, up_part, (((1,), (1,)), ((), ())), preferred_element_type=jnp.float32
        )
    )
    fed = scatter_rows(jnp.dot(active, down_part, preferred_element_type=jnp.float32))
    block_output = (middle + fed + vec_two[2]).reshape(
        slot_count, block_size, model_width
    ) * live_mask

    def outer(left, right):
        return halved(
            lax.dot_general(
                left, right, (((0,), (0,)), ((), ())), preferred_element_type=jnp.float32
            )
        )

    shrink_sum = lax.psum_scatter(
        outer(active, cot_all), "dp", scatter_dimension=0, tiled=True
    ).astype(jnp.float32)
    expand_sum = collect_columns(
        lax.psum_scatter(outer(lifted_two, upper_half), "dp", scatter_dimension=0, tiled=True),
        groups,
        hidden_part,
    ).astype(jnp.float32)
    bias_grad = jnp.sum(upper_grad, axis=0).reshape(replicas, 1, hidden_part)

    gain_two_grad = jnp.sum(lift_two_grad * normed_two, axis=0)
    shift_two_grad = jnp.sum(lift_two_grad, axis=0)
    middle_grad = cotangent + norm_back(lift_two_grad * vec_two[0], normed_two, inverse_two)
    middle_half = halved(middle_grad)
    out_bias_grad = jnp.sum(middle_grad, axis=0)
    middle_cols = lax.all_to_all(
        middle_half.reshape(slot_count, block_size, model_width), "seq", 2, 1, tiled=True
    ).reshape(all_rows, part_width)
    attended_back = halved(
        lax.dot_general(
            middle_cols, out_part, (((1,), (1,)), ((), ())), preferred_element_type=jnp.float32
        )
    )
    attended_grad = to_heads(
        lax.psum_scatter(
            jnp.transpose(attended_back.reshape(all_rows, groups, part_width), (1, 0, 2)),
            "seq",
            scatter_dimension=0,
            tiled=True,
        ).reshape(all_rows, part_width)
    )
    outward_part = outer(attended, middle_cols)
    delta_sum = jnp.sum(
        attended_grad.astype(jnp.float32) * attended_heads.astype(jnp.float32),
        axis=-1,
        keepdims=True,
    )
    weight_grad = jnp.einsum(
        "shqd,shkd->shqk", attended_grad, values, preferred_element_type=jnp.float32
    )
    score_grad = halved(weights_full * (weight_grad - delta_sum) * score_scale)
    query_grad = from_heads(
        jnp.einsum("shqk,shkd->shqd", score_grad, keys, preferred_element_type=jnp.float32)
    )
    key_grad = from_heads(
        jnp.einsum("shqk,shqd->shkd", score_grad, queries, preferred_element_type=jnp.float32)
    )
    value_grad = from_heads(
        jnp.einsum(
            "shqk,shqd->shkd", weights_half, attended_grad, preferred_element_type=jnp.float32
        )
    )
    packed_grad = halved(jnp.concatenate([query_grad, key_grad, value_grad], axis=1))
    lift_one_grad = scatter_rows(
        lax.dot_general(
            packed_grad, in_part, (((1,), (1,)), ((), ())), preferred_element_type=jnp.float32
        )
    )
    inward_part = outer(lifted_one, packed_grad)

    def place_part(part):
        return lax.dynamic_update_slice_in_dim(
            jnp.zeros((model_width,), jnp.float32), part, mine * part_width, 0
        )

    gain_one_grad = jnp.sum(lift_one_grad * normed_one, axis=0)
    shift_one_grad = jnp.sum(lift_one_grad, axis=0)
    tokens_grad = middle_grad + norm_back(lift_one_grad * vec_one[0], normed_one, inverse_one)
    input_gradient = tokens_grad.reshape(slot_count, block_size, model_width) * live_mask
    vector_grads = jnp.stack(
        [
            gain_one_grad,
            shift_one_grad,
            place_part(jnp.sum(query_grad, axis=0)),
            place_part(jnp.sum(value_grad, axis=0)),
            out_bias_grad,
            gain_two_grad,
            shift_two_grad,
            feed_bias_grad,
        ]
    ).reshape(8, devices, vec_width)
    bias_placed = lax.dynamic_update_slice_in_dim(
        jnp.zeros((replicas, groups, hidden_part), jnp.float32), bias_grad, mine, 1
    ).reshape(devices, hidden_part)
    small_grads = halved(
        jnp.concatenate(
            [jnp.transpose(vector_grads, (1, 0, 2)).reshape(devices, 8 * vec_width), bias_placed],
            axis=1,
        )
    ).reshape(replicas, groups, small_size)
    small_grads = jnp.pad(
        small_grads, ((0, 0), (0, pad_rows - groups), (0, model_width - small_size))
    )
    both_grads = jnp.concatenate([inward_part, outward_part], axis=1).reshape(
        replicas, block_rows, model_width
    )
    reduced = lax.psum_scatter(
        jnp.concatenate([both_grads, small_grads], axis=1).reshape(-1, model_width),
        "dp",
        scatter_dimension=0,
        tiled=True,
    )
    returned = lax.all_to_all(
        jnp.concatenate(
            [
                reduced[:block_rows].reshape(groups, in_rows, model_width),
                reduced[block_rows : block_rows + groups].reshape(groups, 1, model_width),
            ],
            axis=1,
        ),
        "seq",
        0,
        0,
        tiled=True,
    )
    both_sum = jnp.transpose(
        returned[:, :in_rows].reshape(groups, in_rows, -1, part_width), (1, 2, 0, 3)
    ).reshape(in_rows, -1).astype(jnp.float32)
    inward_sum = both_sum[:, : 3 * model_width]
    outward_sum = both_sum[:, 3 * model_width :]
    small_sum = jnp.sum(returned[:, in_rows, :small_size].astype(jnp.float32), axis=0)
    vector_sum = small_sum[: 8 * vec_width].reshape(8, vec_width)
    attend_vec_sum = vector_sum[:5]
    feed_vec_sum = vector_sum[5:]
    bias_sum = small_sum[8 * vec_width :]
    inward_new, inward_state = adamw_update(inward, inward_sum, inward_moments, weight_decay)
    outward_new, outward_state = adamw_update(outward, outward_sum, outward_moments, weight_decay)
    attend_new, attend_state = adamw_update(attend_vectors, attend_vec_sum, attend_moments, 0.0)
    expand_new, expand_state = adamw_update(expand, expand_sum, expand_moments, weight_decay)
    shrink_new, shrink_state = adamw_update(shrink, shrink_sum, shrink_moments, weight_decay)
    feed_new, feed_state = adamw_update(feed_vectors, feed_vec_sum, feed_moments, 0.0)
    bias_new, bias_state = adamw_update(expand_bias, bias_sum, bias_moments, 0.0)
    return (
        block_output,
        input_gradient,
        inward_sum,
        outward_sum,
        attend_vec_sum,
        expand_sum,
        shrink_sum,
        feed_vec_sum,
        bias_sum,
        inward_new,
        outward_new,
        attend_new,
        expand_new,
        shrink_new,
        feed_new,
        bias_new,
        inward_state,
        outward_state,
        attend_state,
        expand_state,
        shrink_state,
        feed_state,
        bias_state,
    )


MESH = pl.DeviceIdType.MESH
copy_slots = 160


def mm(left, right):
    return lax.dot_general(
        left, right, (((1,), (0,)), ((), ())), preferred_element_type=jnp.float32
    )


def mm_nt(left, right):
    return lax.dot_general(
        left, right, (((1,), (1,)), ((), ())), preferred_element_type=jnp.float32
    )


def mm_tn(left, right):
    return lax.dot_general(
        left, right, (((0,), (0,)), ((), ())), preferred_element_type=jnp.float32
    )


def wide(operand):
    return operand.astype(jnp.float32)


def scratch_plan(slots, length, block, width, head_count, in_rows, hidden):
    half, full = jnp.bfloat16, jnp.float32
    rows = slots * block
    part = head_count * HEAD_DIM
    dp_rows = in_rows * 4
    pairs = slots * head_count
    return dict(
        s_in=((4, in_rows, 3 * part), half),
        s_up=((4, in_rows, hidden), half),
        in_all=((width, 4 * part), half),
        up_all=((width, hidden), half),
        down_all=((hidden, width), half),
        out_ring=((4, 2, in_rows, width), half),
        out_all=((4, 2, in_rows, width), half),
        live=((rows, 1), full),
        small=((16, 128), full),
        small_land=((4, 8, 128), full),
        small_all=((8, 16, 128), full),
        vecs=((16, width), full),
        normed_one=((rows, width), full),
        inverse_one=((rows, 1), full),
        lifted_one=((slots, length, width), half),
        cot_all=((slots, length, width), half),
        q_h=((pairs, length, HEAD_DIM), half),
        k_h=((pairs, length, HEAD_DIM), half),
        v_h=((pairs, length, HEAD_DIM), half),
        weights=((pairs, length, length), full),
        att_h=((pairs, length, HEAD_DIM), half),
        attended=((slots, length, part), half),
        proj_p=((slots, length, width), half),
        proj_c=((2, slots, block, width), half),
        proj_b=((slots, block, width), half),
        proj_y=((slots, block, width), half),
        middle=((rows, width), full),
        normed_two=((rows, width), full),
        inverse_two=((rows, 1), full),
        lifted_two=((slots, length, width), half),
        active=((slots, length, hidden), half),
        slope=((slots, length, hidden), full),
        upper_half=((slots, length, hidden), half),
        two_p=((slots, length, width), half),
        two_c=((2, slots, block, width), half),
        two_b=((slots, block, width), half),
        two_y=((slots, block, width), half),
        fed_p=((slots, length, width), half),
        fed_c=((2, slots, block, width), half),
        fed_b=((slots, block, width), half),
        fed_y=((slots, block, width), half),
        one_p=((slots, length, width), half),
        one_c=((2, slots, block, width), half),
        one_b=((slots, block, width), half),
        one_y=((slots, block, width), half),
        mid_all=((slots, length, width), half),
        mid_grad=((rows, width), full),
        ag_h=((pairs, length, HEAD_DIM), half),
        pg_h=((3, pairs, length, HEAD_DIM), half),
        bias_h=((2, pairs, 1, HEAD_DIM), full),
        pg=((slots, length, 3 * part), half),
        sh_s=((2, 4, dp_rows, width), half),
        sh_l=((2, 4, dp_rows, width), half),
        ex_s=((2, 4, dp_rows, hidden), half),
        ex_l=((2, 4, dp_rows, hidden), half),
        ex_f=((dp_rows, hidden), half),
        ex_g=((4, in_rows, hidden), half),
        in_s=((2, 4, dp_rows, 4 * part), half),
        in_l=((2, 4, dp_rows, 4 * part), half),
        in_f=((dp_rows, 3 * part), half),
        in_g=((4, in_rows, 3 * part), half),
        og=((4, 2, in_rows, width), half),
        og_ring=((4, 2, in_rows, width), half),
        g_full=((16, width), full),
        g_out=((2, 4, 16, 128), full),
        g_l=((4, 16, 128), full),
        g_z=((3, 16, 128), full),
        g_f=((8, 128), full),
        g_g=((4, 8, 128), full),
    )


def layer_kernel(names, *refs):
    r = types.SimpleNamespace(**dict(zip(names, refs)))
    ssem, rsem = r.ssem, r.rsem
    slots, length, width = r.lifted_one.shape
    rows = r.middle.shape[0]
    block = rows // slots
    pairs = r.q_h.shape[0]
    heads = pairs // slots
    part = heads * HEAD_DIM
    in_rows = r.outward.shape[0]
    dp_rows = 4 * in_rows
    hidden = r.up_all.shape[1]
    score_scale = 1.0 / math.sqrt(HEAD_DIM)

    dp, me = lax.axis_index("dp"), lax.axis_index("seq")
    z, x = dp // 2, dp % 2
    y, core = me // 2, me % 2
    sib = me + 1 - 2 * core
    yp = (me + 2) % 4
    xdp = dp + 1 - 2 * x
    turn = y + 2 * core

    def z_dp(k):
        return 2 * ((z + k) % 4) + x

    place = (1 - x) * z + x * (7 - z)

    def ring_dp(k):
        at = (place + k + 8) % 8
        return (1 - at // 4) * 2 * at + (at // 4) * (15 - 2 * at)

    right, left = (ring_dp(1), me), (ring_dp(-1), me)

    used = [0]
    sent = []

    def slot():
        used[0] += 1
        return used[0] - 1

    def rc(source, target, device, at=None, start=True):
        index = slot() if at is None else at
        copy = pltpu.make_async_remote_copy(
            source,
            target,
            ssem.at[index],
            rsem.at[index],
            device_id=device,
            device_id_type=MESH,
        )
        if start:
            copy.start()
            if at is None:
                sent.append(copy)
        return copy

    barrier = pltpu.get_barrier_semaphore()
    for device in (
        [(dp, (me + k) % 4) for k in (1, 2, 3)]
        + [(z_dp(k), me) for k in (1, 2, 3)]
        + [(xdp, me)]
    ):
        pl.semaphore_signal(barrier, inc=1, device_id=device, device_id_type=MESH)

    def seq_rows(which):
        return pl.ds(which * block, block)

    class SeqGather:
        def __init__(self, buf):
            self.buf = buf
            own = seq_rows(me)
            self.far = [rc(buf.at[s, own], buf.at[s, own], (dp, yp)) for s in range(slots)]
            self.near = rc(buf.at[:, own], buf.at[:, own], (dp, sib))

        def forward(self):
            theirs = seq_rows(yp)
            self.passed = []
            for s in range(slots):
                self.far[s].wait_recv()
                self.passed.append(
                    rc(self.buf.at[s, theirs], self.buf.at[s, theirs], (dp, sib))
                )

        def finish(self):
            self.near.wait_recv()
            for copy in self.passed:
                copy.wait_recv()

    class SeqScatter:
        def __init__(self, partial, near, sums, far):
            self.p, self.c, self.b, self.y = partial, near, sums, far
            self.base = slot()
            slot()

        def near_copy(self, index, which):
            return rc(
                self.p.at[:, seq_rows(which)],
                self.c.at[1 - index],
                (dp, sib),
                at=self.base + index,
                start=False,
            )

        def order(self, index):
            return (me + (1 - index // 2) * (sib - me) + 2 * (1 - index % 2)) % 4

        def fill(self, compute):
            def step(index, carry):
                which = self.order(index)
                value = compute(which)
                self.p[:, seq_rows(which)] = halved(value).reshape(slots, block, width)

                @pl.when(index < 2)
                def _():
                    self.near_copy(index, which).start()

                return carry

            lax.fori_loop(0, 4, step, 0)
            for index in range(2):
                sent.append(self.near_copy(index, self.order(index)))

        def middle(self):
            self.near_copy(0, self.order(0)).wait_recv()
            self.far = []
            for s in range(slots):
                self.b[s] = halved(wide(self.p[s, seq_rows(yp)]) + wide(self.c[1, s]))
                self.far.append(rc(self.b.at[s], self.y.at[s], (dp, yp)))

        def finish(self):
            self.near_copy(1, self.order(1)).wait_recv()
            for copy in self.far:
                copy.wait_recv()
            total = wide(self.p[:, seq_rows(me)]) + wide(self.c[0]) + wide(self.y[...])
            return total.reshape(rows, width)

    class SmallGather:
        def __init__(self, buf):
            self.buf = buf

        def send(self):
            own = self.buf.at[dp]
            self.far = [rc(own, own, (z_dp(k), me)) for k in (1, 2, 3)]
            self.near = [rc(own, own, (xdp, me))]

        def forward(self):
            for k in (1, 2, 3):
                self.far[k - 1].wait_recv()
                theirs = self.buf.at[z_dp(4 - k)]
                self.near.append(rc(theirs, theirs, (xdp, me)))

        def finish(self):
            for copy in self.near:
                copy.wait_recv()

    half_rows = dp_rows // 2

    class RingGather:
        def __init__(self, buf):
            self.buf, self.moving = buf, []

        def at(self, which, piece=None):
            start = which * dp_rows
            if piece is None:
                return self.buf.at[pl.ds(pl.multiple_of(start, dp_rows), dp_rows)]
            start = start + piece * half_rows
            return self.buf.at[pl.ds(pl.multiple_of(start, half_rows), half_rows)]

        def step(self, j):
            self.finish()
            ahead = self.at(ring_dp(1 - j), 0 if j == 4 else None)
            back = self.at(ring_dp(j - 1), 1 if j == 4 else None)
            self.moving = [rc(ahead, ahead, right), rc(back, back, left)]

        def finish(self):
            for copy in self.moving:
                copy.wait_recv()

    class RingScatter:
        def __init__(self, chunk, away, land):
            self.chunk, self.away, self.land, self.moving = chunk, away, land, []

        def arrive(self):
            for copy in self.moving:
                copy.wait_recv()

        def step(self, j):
            if j == 1:
                value = halved(self.chunk(ring_dp(4)))
                here = slice(0, half_rows)
                self.away[0, 0, here] = value[:half_rows]
                self.away[1, 0, here] = value[half_rows:]
                rows_sent = pl.ds(0, half_rows)
            else:
                ahead, back = self.chunk(ring_dp(5 - j)), self.chunk(ring_dp(j - 5))
                self.arrive()
                if j == 2:
                    near = wide(self.land[0, 0, 0:half_rows])
                    far = wide(self.land[1, 0, 0:half_rows])
                    self.away[0, 1, 0:half_rows] = halved(ahead[:half_rows] + near)
                    self.away[0, 1, half_rows:dp_rows] = halved(ahead[half_rows:])
                    self.away[1, 1, 0:half_rows] = halved(back[:half_rows])
                    self.away[1, 1, half_rows:dp_rows] = halved(back[half_rows:] + far)
                else:
                    self.away[0, j - 1] = halved(ahead + wide(self.land[0, j - 2]))
                    self.away[1, j - 1] = halved(back + wide(self.land[1, j - 2]))
                rows_sent = pl.ds(0, dp_rows)
            self.moving = [
                rc(
                    self.away.at[way, j - 1, rows_sent],
                    self.land.at[way, j - 1, rows_sent],
                    target,
                )
                for way, target in ((0, right), (1, left))
            ]

        def finish(self):
            own = self.chunk(dp)
            self.arrive()
            return own + (wide(self.land[0, 3]) + wide(self.land[1, 3]))

    def chunk_of(left_ref, right_ref):
        def chunk(which):
            at = pl.ds(pl.multiple_of(which * dp_rows, dp_rows), dp_rows)
            return mm_tn(
                left_ref[:, :, at].reshape(-1, dp_rows), right_ref[...].reshape(slots * length, -1)
            )

        return chunk

    vec_width = r.attend_vectors.shape[1]
    r.small[0:5, 0:vec_width] = r.attend_vectors[...]
    r.small[5:8, 0:vec_width] = r.feed_vectors[...]
    spread = jnp.concatenate([r.small[0:8, 0:vec_width]] * 4, axis=1)
    lane = lax.broadcasted_iota(jnp.int32, spread.shape, 1)
    r.small[0:8] = wide(halved(jnp.where(lane // vec_width == me, spread, 0.0)))
    r.small[8:16] = jnp.broadcast_to(wide(halved(r.expand_bias[...])), (8, 128))
    for s in range(slots):
        found = jnp.int32(0)
        for i in range(r.placement.shape[0]):
            found = jnp.where(r.placement[i] == dp * slots + s, 1, found)
        r.live[s * block : (s + 1) * block] = jnp.full((block, 1), found.astype(jnp.float32))

    dp_at = pl.ds(pl.multiple_of(dp * dp_rows, dp_rows), dp_rows)
    own_at = pl.ds(pl.multiple_of(dp * dp_rows + me * in_rows, in_rows), in_rows)
    r.down_all[dp_at] = halved(r.shrink[...])
    r.small_land[0] = r.small[0:8]
    down, inward, up = RingGather(r.down_all), RingGather(r.in_all), RingGather(r.up_all)
    pl.semaphore_wait(barrier, 7)
    down.step(1)
    small_seq = [
        rc(r.small_land.at[0], r.small_land.at[k], (dp, (me + k) % 4)) for k in (1, 2, 3)
    ]

    for g in range(4):
        turn_g = g // 2 + 2 * (g % 2)
        for third in range(3):
            pieces = [
                r.inward[:, pl.ds(third * width + (4 * j + turn_g) * HEAD_DIM, HEAD_DIM)]
                for j in range(heads)
            ]
            r.s_in[g, :, third * part : (third + 1) * part] = halved(
                jnp.concatenate(pieces, axis=1)
            )
    in_at = r.in_all.at[own_at, pl.ds(0, 3 * part)]
    in_seq = [
        rc(r.s_in.at[(me + k) % 4], in_at, (dp, (me + k) % 4)) for k in (2, 3, 1)
    ]
    in_at[...] = r.s_in[me]
    for i in range(4):
        rows_at = pl.ds(pl.multiple_of(dp * dp_rows + i * in_rows, in_rows), in_rows)
        r.in_all[rows_at, 3 * part : 4 * part] = halved(r.outward[:, i * part : (i + 1) * part])
    for g in range(4):
        for d in range(hidden // 128):
            r.s_up[g, :, d * 128 : (d + 1) * 128] = halved(
                r.expand[:, pl.ds((d * 4 + g) * 128, 128)]
            )
    up_seq = [
        rc(r.s_up.at[(me + k) % 4], r.up_all.at[own_at], (dp, (me + k) % 4))
        for k in (2, 3, 1)
    ]
    r.up_all[own_at] = r.s_up[me]

    normed, inverse = normalize(r.tokens[...])
    r.normed_one[...] = normed
    r.inverse_one[...] = inverse
    cotangent = r.cot[...] * r.live[...]
    r.cot_all[:, seq_rows(me)] = halved(cotangent).reshape(slots, block, width)

    for copy in small_seq:
        copy.wait_recv()
    mine_small = r.small_all.at[dp]
    mine_small[0:8] = (r.small_land[0] + r.small_land[1]) + (
        r.small_land[2] + r.small_land[3]
    )
    mine_small[8:16] = r.small[8:16]
    small = SmallGather(r.small_all)
    small.send()

    for copy in in_seq:
        copy.wait_recv()
    inward.step(1)
    for copy in up_seq:
        copy.wait_recv()
    up.step(1)
    small.forward()
    small.finish()
    for d in range(8):
        r.vecs[:, d * 128 : (d + 1) * 128] = r.small_all[d]

    def vec(index):
        return r.vecs[index : index + 1, :]

    r.lifted_one[:, seq_rows(me)] = halved(
        r.normed_one[...] * vec(0) + vec(1)
    ).reshape(slots, block, width)
    lift_one = SeqGather(r.lifted_one)

    inward.step(2)
    up.step(2)
    lift_one.forward()
    cot = SeqGather(r.cot_all)
    inward.step(3)
    up.step(3)
    cot.forward()
    inward.step(4)
    up.step(4)
    lift_one.finish()
    inward.finish()
    down.step(2)
    for d in range(8):
        r.out_ring[d // 2, d % 2] = jnp.concatenate(
            [
                r.in_all[d * dp_rows + i * in_rows : d * dp_rows + (i + 1) * in_rows, 3 * part :]
                for i in range(4)
            ],
            axis=1,
        )
    r.out_all[:, core] = r.out_ring[:, core]
    out_pair = rc(r.out_ring.at[:, 1 - core], r.out_all.at[:, core], (dp, sib))

    def own_heads(row):
        pieces = []
        for j in range(heads):
            piece = jnp.zeros((1, HEAD_DIM), jnp.float32)
            for t in range(4):
                start = (4 * j + t) * HEAD_DIM
                piece = jnp.where(turn == t, row[:, start : start + HEAD_DIM], piece)
            pieces.append(piece)
        return jnp.concatenate(pieces, axis=1)

    bias_query, bias_value = own_heads(vec(2)), own_heads(vec(3))

    def project_in(s, carry):
        packed = mm(r.lifted_one[s], r.in_all[:, : 3 * part])
        queries = halved(packed[:, :part] + bias_query)
        keys = halved(packed[:, part : 2 * part])
        values = halved(packed[:, 2 * part :] + bias_value)
        for j in range(heads):
            cut = slice(j * HEAD_DIM, (j + 1) * HEAD_DIM)
            r.q_h[s * heads + j] = queries[:, cut]
            r.k_h[s * heads + j] = keys[:, cut]
            r.v_h[s * heads + j] = values[:, cut]
        return carry

    lax.fori_loop(0, slots, project_in, 0)

    def attend(p, carry):
        scores = mm_nt(r.q_h[p], r.k_h[p]) * score_scale
        row_at = lax.broadcasted_iota(jnp.int32, scores.shape, 0)
        column_at = lax.broadcasted_iota(jnp.int32, scores.shape, 1)
        scores = jnp.where(column_at <= row_at, scores, masked_score)
        peak = jnp.max(scores, axis=-1, keepdims=True)
        raised = jnp.exp(scores - peak)
        weights = raised * (1.0 / jnp.sum(raised, axis=-1, keepdims=True))
        r.weights[p] = weights
        r.att_h[p] = halved(mm(halved(weights), r.v_h[p]))
        return carry

    lax.fori_loop(0, pairs, attend, 0)
    for s in range(slots):
        r.attended[s] = jnp.concatenate(
            [r.att_h[s * heads + j] for j in range(heads)], axis=1
        )

    down.step(3)
    out_pair.wait_recv()
    proj = SeqScatter(r.proj_p, r.proj_c, r.proj_b, r.proj_y)
    proj.fill(
        lambda which: mm(
            r.attended[:, seq_rows(which)].reshape(rows, part), r.out_all[...].reshape(part, width)
        )
    )
    proj.middle()
    middle = r.tokens[...] + proj.finish() + vec(4)
    r.middle[...] = middle
    normed, inverse = normalize(middle)
    r.normed_two[...] = normed
    r.inverse_two[...] = inverse
    r.lifted_two[:, seq_rows(me)] = halved(normed * vec(5) + vec(6)).reshape(
        slots, block, width
    )
    lift_two = SeqGather(r.lifted_two)
    lift_two.forward()
    down.step(4)
    lift_two.finish()
    cot.finish()
    up.finish()

    def feed(index, carry):
        here = seq_rows(index)
        upper = mm(r.lifted_two[:, here].reshape(rows, width), r.up_all[...]) + vec(8)
        active, slope = gelu_pair(upper)
        r.active[:, here] = halved(active).reshape(slots, block, hidden)
        r.slope[:, here] = slope.reshape(slots, block, hidden)
        return carry

    lax.fori_loop(0, 4, feed, 0)
    shrink = RingScatter(chunk_of(r.active, r.cot_all), r.sh_s, r.sh_l)
    shrink.step(1)
    down.finish()

    two = SeqScatter(r.two_p, r.two_c, r.two_b, r.two_y)
    r.g_full[8:9, :] = jnp.zeros((1, hidden), jnp.float32)

    def feed_back(which):
        here = seq_rows(which)
        upper_grad = mm_nt(
            r.cot_all[:, here].reshape(rows, width), r.down_all[...]
        ) * r.slope[:, here].reshape(rows, hidden)
        r.g_full[8:9, :] += jnp.sum(upper_grad, axis=0, keepdims=True)
        upper_half = halved(upper_grad)
        r.upper_half[:, here] = upper_half.reshape(slots, block, hidden)
        return mm_nt(upper_half, r.up_all[...])

    two.fill(feed_back)
    two.middle()
    expand = RingScatter(chunk_of(r.lifted_two, r.upper_half), r.ex_s, r.ex_l)
    expand.step(1)
    shrink.step(2)
    fed = SeqScatter(r.fed_p, r.fed_c, r.fed_b, r.fed_y)
    fed.fill(
        lambda which: mm(r.active[:, seq_rows(which)].reshape(rows, hidden), r.down_all[...])
    )
    lift_grad = two.finish()
    normed = r.normed_two[...]
    r.g_full[5:6, :] = jnp.sum(lift_grad * normed, axis=0, keepdims=True)
    r.g_full[6:7, :] = jnp.sum(lift_grad, axis=0, keepdims=True)
    cotangent = r.cot[...] * r.live[...]
    r.g_full[7:8, :] = jnp.sum(cotangent, axis=0, keepdims=True)
    middle_grad = cotangent + norm_back(lift_grad * vec(5), normed, r.inverse_two[...])
    r.mid_grad[...] = middle_grad
    r.g_full[4:5, :] = jnp.sum(middle_grad, axis=0, keepdims=True)
    r.mid_all[:, seq_rows(me)] = halved(middle_grad).reshape(slots, block, width)
    mid = SeqGather(r.mid_all)
    expand.step(2)
    mid.forward()
    shrink.step(3)
    fed.middle()
    mid.finish()

    for s in range(slots):
        grads = halved(mm_nt(r.mid_all[s], r.out_all[...].reshape(part, width)))
        for j in range(heads):
            r.ag_h[s * heads + j] = grads[:, j * HEAD_DIM : (j + 1) * HEAD_DIM]

    r.og[...] = halved(
        mm_tn(
            r.attended[...].reshape(slots * length, part),
            r.mid_all[...].reshape(slots * length, width),
        )
    ).reshape(4, 2, in_rows, width)
    r.og_ring[:, core] = r.og[:, core]
    og_pair = rc(r.og.at[:, 1 - core], r.og_ring.at[:, core], (dp, sib))
    expand.step(3)
    shrink.step(4)

    def attend_back(p, carry):
        weights, grads = r.weights[p], r.ag_h[p]
        delta = jnp.sum(wide(grads) * wide(r.att_h[p]), axis=-1, keepdims=True)
        weight_grad = mm_nt(grads, r.v_h[p])
        score_grad = halved(weights * (weight_grad - delta) * score_scale)
        query_grad = mm(score_grad, r.k_h[p])
        key_grad = mm_tn(score_grad, r.q_h[p])
        value_grad = mm_tn(halved(weights), grads)
        r.bias_h[0, p] = jnp.sum(query_grad, axis=0, keepdims=True)
        r.bias_h[1, p] = jnp.sum(value_grad, axis=0, keepdims=True)
        r.pg_h[0, p] = halved(query_grad)
        r.pg_h[1, p] = halved(key_grad)
        r.pg_h[2, p] = halved(value_grad)
        return carry

    lax.fori_loop(0, pairs, attend_back, 0)
    for s in range(slots):
        r.pg[s] = jnp.concatenate(
            [r.pg_h[i, s * heads + j] for i in range(3) for j in range(heads)], axis=1
        )
    expand.step(4)
    og_pair.wait_recv()

    def inner_chunk(which):
        ours = r.og_ring[which // 2, which % 2]
        packed = jnp.concatenate(
            [ours[:, i * part : (i + 1) * part] for i in range(4)], axis=0
        )
        return jnp.concatenate([chunk_of(r.lifted_one, r.pg)(which), wide(packed)], axis=1)

    inner = RingScatter(inner_chunk, r.in_s, r.in_l)
    inner.step(1)
    one = SeqScatter(r.one_p, r.one_c, r.one_b, r.one_y)
    one.fill(
        lambda which: mm_nt(
            r.pg[:, seq_rows(which)].reshape(rows, 3 * part), r.in_all[:, : 3 * part]
        )
    )
    one.middle()
    inner.step(2)

    block_output = r.middle[...] + fed.finish() + vec(7)
    r.block_output[...] = block_output * r.live[...]
    r.shrink_sum[...] = shrink.finish()
    lift_grad = one.finish()
    normed = r.normed_one[...]
    r.g_full[0:1, :] = jnp.sum(lift_grad * normed, axis=0, keepdims=True)
    r.g_full[1:2, :] = jnp.sum(lift_grad, axis=0, keepdims=True)
    input_gradient = r.mid_grad[...] + norm_back(
        lift_grad * vec(0), normed, r.inverse_one[...]
    )
    r.input_gradient[...] = input_gradient * r.live[...]
    for i in range(2):
        pieces = []
        for head in range(4 * heads):
            total = jnp.zeros((1, HEAD_DIM), jnp.float32)
            for s in range(slots):
                total = total + r.bias_h[i, s * heads + head // 4]
            pieces.append(jnp.where(turn == head % 4, total, 0.0))
        r.g_full[2 + i : 3 + i, :] = jnp.concatenate(pieces, axis=1)
    r.g_full[9:16, :] = jnp.zeros((7, width), jnp.float32)
    for d in range(8):
        r.g_out[d % 2, d // 2] = r.g_full[:, d * 128 : (d + 1) * 128]
    g_near = rc(r.g_out.at[1 - x], r.g_l, (xdp, me))

    inner.step(3)
    g_near.wait_recv()
    r.g_l[...] = r.g_l[...] + r.g_out[x]
    g_far = [rc(r.g_l.at[(z + k) % 4], r.g_z.at[k - 1], (z_dp(k), me)) for k in (1, 2, 3)]

    r.ex_f[...] = halved(expand.finish())

    def sub(buf, which):
        return buf.at[pl.ds(pl.multiple_of(which * in_rows, in_rows), in_rows)]

    def seq_return(buf, land):
        land[0] = buf[pl.ds(pl.multiple_of(me * in_rows, in_rows), in_rows)]
        return [
            rc(sub(buf, (me + k) % 4), land.at[k], (dp, (me + k) % 4)) for k in (2, 3, 1)
        ]

    ex_back = seq_return(r.ex_f, r.ex_g)
    inner.step(4)
    for copy in g_far:
        copy.wait_recv()
    g_total = r.g_l[z] + r.g_z[0] + r.g_z[1] + r.g_z[2]
    r.g_f[...] = g_total[0:8]
    r.g_g[0] = g_total[0:8]
    g_back = [rc(r.g_f, r.g_g.at[k], (dp, (me + k) % 4)) for k in (1, 2, 3)]

    for copy in ex_back:
        copy.wait_recv()
    for k in range(4):
        for g in range(4):

            @pl.when((me - k + 4) % 4 == g)
            def _():
                value = wide(r.ex_g[k])
                for d in range(hidden // 128):
                    start = (d * 4 + g) * 128
                    r.expand_sum[:, start : start + 128] = value[:, d * 128 : (d + 1) * 128]

    inner_sum = inner.finish()
    r.in_f[...] = halved(inner_sum[:, : 3 * part])
    for i in range(4):
        r.outward_sum[:, i * part : (i + 1) * part] = inner_sum[
            i * in_rows : (i + 1) * in_rows, 3 * part :
        ]
    in_back = seq_return(r.in_f, r.in_g)
    for copy in g_back:
        copy.wait_recv()
    r.small_sum[0:8] = (r.g_g[0] + r.g_g[1]) + (r.g_g[2] + r.g_g[3])
    r.small_sum[8:16] = g_total[8:16]
    for copy in in_back:
        copy.wait_recv()
    by_seq = []
    for g in range(4):
        by_seq.append(r.in_g[(me - g + 4) % 4])
    for third in range(3):
        pieces = []
        for head in range(4 * heads):
            g = 2 * (head % 2) + (head // 2) % 2
            start = third * part + (head // 4) * HEAD_DIM
            pieces.append(by_seq[g][:, start : start + HEAD_DIM])
        r.inward_sum[:, third * width : (third + 1) * width] = wide(
            jnp.concatenate(pieces, axis=1)
        )

    for copy in sent:
        copy.wait_send()


def adamw_kernel(decays, count, *refs):
    kinds = len(decays)
    masters, sums, moments = refs[:kinds], refs[kinds : 2 * kinds], refs[2 * kinds : 3 * kinds]
    passed = refs[3 * kinds : 3 * kinds + count]
    outs = refs[3 * kinds + count :]
    for i, decay in enumerate(decays):
        gradient = sums[i][...]
        fresh, state = outs[kinds + i], outs[2 * kinds + i]
        first_moment = beta_first * moments[i][0] + (1.0 - beta_first) * gradient
        second = beta_second * moments[i][1] + (1.0 - beta_second) * gradient * gradient
        unbiased_first = first_moment * (1.0 / (1.0 - beta_first**adam_steps))
        unbiased_second = second * (1.0 / (1.0 - beta_second**adam_steps))
        update = unbiased_first / (jnp.sqrt(unbiased_second) + adam_epsilon)
        parameter = masters[i][...]
        fresh[...] = parameter - learn_rate * (update + decay * parameter)
        state[0] = first_moment
        state[1] = second
        outs[i][...] = gradient
    for i in range(count):
        outs[3 * kinds + i][...] = passed[i][...]


def adamw_call(masters, sums, moments, decays, passed, steps):
    def spec(array):
        axis = array.ndim - 2
        small = array.shape[axis] % (8 * steps) != 0
        block = list(array.shape)
        if not small:
            block[axis] //= steps

        def index(i):
            place = [0] * array.ndim
            if not small:
                place[axis] = i
            return tuple(place)

        return pl.BlockSpec(tuple(block), index)

    arrays = [*masters, *sums, *moments, *passed]
    results = [*sums, *masters, *moments, *passed]
    return pl.pallas_call(
        functools.partial(adamw_kernel, decays, len(passed)),
        grid=(steps,),
        out_shape=[jax.ShapeDtypeStruct(array.shape, jnp.float32) for array in results],
        in_specs=[spec(array) for array in arrays],
        out_specs=[spec(array) for array in results],
        compiler_params=pltpu.CompilerParams(vmem_limit_bytes=60 * 2**20),
        name="adamw",
    )(*arrays)


def fast_body(
    tokens,
    output_cotangent,
    placement,
    inward,
    outward,
    attend_vectors,
    expand,
    shrink,
    feed_vectors,
    expand_bias,
    *moments,
):
    slot_count, block_size, model_width = tokens.shape
    groups = lax.axis_size("seq")
    mine = lax.axis_index("seq")
    row_count = slot_count * block_size
    hidden_part = expand.shape[1] // groups
    vec_width = attend_vectors.shape[1]
    in_rows = inward.shape[0]

    plan = scratch_plan(
        slot_count,
        block_size * groups,
        block_size,
        model_width,
        HEADS // groups,
        in_rows,
        hidden_part,
    )
    inputs = dict(
        tokens=tokens.reshape(row_count, model_width),
        cot=output_cotangent.reshape(row_count, model_width),
        placement=placement,
        attend_vectors=attend_vectors,
        feed_vectors=feed_vectors,
        expand_bias=expand_bias.reshape(1, -1),
        inward=inward,
        outward=outward,
        expand=expand,
        shrink=shrink,
    )
    outputs = dict(
        block_output=(row_count, model_width),
        input_gradient=(row_count, model_width),
        inward_sum=inward.shape,
        outward_sum=outward.shape,
        expand_sum=expand.shape,
        shrink_sum=shrink.shape,
        small_sum=(16, 128),
    )
    names = list(inputs) + list(outputs) + list(plan) + ["ssem", "rsem"]
    found = pl.pallas_call(
        functools.partial(layer_kernel, names),
        out_shape=[jax.ShapeDtypeStruct(shape, jnp.float32) for shape in outputs.values()],
        in_specs=[
            pl.BlockSpec(memory_space=pltpu.SMEM if name == "placement" else pltpu.VMEM)
            for name in inputs
        ],
        out_specs=[pl.BlockSpec(memory_space=pltpu.VMEM)] * len(outputs),
        scratch_shapes=[pltpu.VMEM(shape, kind) for shape, kind in plan.values()]
        + [pltpu.SemaphoreType.DMA((copy_slots,)), pltpu.SemaphoreType.DMA((copy_slots,))],
        compiler_params=pltpu.CompilerParams(
            collective_id=0, has_side_effects=True, vmem_limit_bytes=60 * 2**20
        ),
        name="layer",
    )(*inputs.values())
    found = types.SimpleNamespace(**dict(zip(outputs, found)))
    vector_sum = lax.dynamic_slice_in_dim(found.small_sum[:8], mine * vec_width, vec_width, 1)
    sums = (
        found.inward_sum,
        found.outward_sum,
        vector_sum[:5],
        found.expand_sum,
        found.shrink_sum,
        vector_sum[5:],
        found.small_sum[8],
    )
    masters = (inward, outward, attend_vectors, expand, shrink, feed_vectors, expand_bias)
    decays = (weight_decay, weight_decay, 0.0, weight_decay, weight_decay, 0.0, 0.0)
    flat = [
        array.reshape(array.shape[:-1] + (1, -1)) if array.shape[-1:] == array.shape[axis:] else array
        for group, axis in ((masters, 0), (sums, 0), (moments, 1))
        for array in group
    ]
    kinds = len(masters)
    done = adamw_call(
        flat[:kinds],
        flat[kinds : 2 * kinds],
        flat[2 * kinds :],
        decays,
        (found.block_output, found.input_gradient),
        4,
    )
    wanted = [*sums, *masters, *moments, tokens, tokens]
    done = [array.reshape(other.shape) for array, other in zip(done, wanted)]
    return (*done[3 * kinds :], *done[: 3 * kinds])


def solution(mesh):
    chosen = fast_body if (mesh.shape["dp"], mesh.shape["seq"]) == (8, 4) else body
    placed = (
        P("dp", "seq", None),
        P("dp", "seq", None),
        P(),
        P(("dp", "seq"), None),
        P(("dp", "seq"), None),
        P(None, ("dp", "seq")),
        P(("dp", "seq"), None),
        P(("dp", "seq"), None),
        P(None, ("dp", "seq")),
        P(("dp", "seq")),
        P(None, ("dp", "seq"), None),
        P(None, ("dp", "seq"), None),
        P(None, None, ("dp", "seq")),
        P(None, ("dp", "seq"), None),
        P(None, ("dp", "seq"), None),
        P(None, None, ("dp", "seq")),
        P(None, ("dp", "seq")),
    )
    return jax.shard_map(
        chosen,
        mesh=mesh,
        in_specs=placed,
        out_specs=(
            P("dp", "seq", None),
            P("dp", "seq", None),
            P(("dp", "seq"), None),
            P(("dp", "seq"), None),
            P(None, ("dp", "seq")),
            P(("dp", "seq"), None),
            P(("dp", "seq"), None),
            P(None, ("dp", "seq")),
            P(("dp", "seq")),
            P(("dp", "seq"), None),
            P(("dp", "seq"), None),
            P(None, ("dp", "seq")),
            P(("dp", "seq"), None),
            P(("dp", "seq"), None),
            P(None, ("dp", "seq")),
            P(("dp", "seq")),
            P(None, ("dp", "seq"), None),
            P(None, ("dp", "seq"), None),
            P(None, None, ("dp", "seq")),
            P(None, ("dp", "seq"), None),
            P(None, ("dp", "seq"), None),
            P(None, None, ("dp", "seq")),
            P(None, ("dp", "seq")),
        ),
        check_vma=False,
    )
```

```python
import functools
import math
import types

import jax
import jax.numpy as jnp
from jax import lax
from jax.experimental import pallas as pl
from jax.experimental.pallas import tpu as pltpu
from jax.sharding import PartitionSpec as P

HEADS = 16
HEAD_DIM = 64


norm_epsilon = 1e-05
beta_first = 0.9
beta_second = 0.95
adam_epsilon = 1e-08
learn_rate = 0.01
weight_decay = 0.1
adam_steps = 4
gelu_scale = 0.7978845608028654
gelu_cubic = 0.044715
masked_score = -1e30


def halved(operand):
    return operand.astype(jnp.bfloat16)


def normalize(operand):
    average = jnp.mean(operand, axis=-1, keepdims=True)
    centered = operand - average
    variance = jnp.mean(centered * centered, axis=-1, keepdims=True)
    inverse = lax.rsqrt(variance + norm_epsilon)
    return (centered * inverse, inverse)


def norm_back(upstream, normed, inverse):
    first_mean = jnp.mean(upstream, axis=-1, keepdims=True)
    second_mean = jnp.mean(upstream * normed, axis=-1, keepdims=True)
    return inverse * (upstream - first_mean - normed * second_mean)


def gelu_pair(upper):
    inner_arg = gelu_scale * (upper + gelu_cubic * upper * upper * upper)
    tangent = jnp.tanh(inner_arg)
    active = 0.5 * upper * (1.0 + tangent)
    slope = 0.5 * (1.0 + tangent) + 0.5 * upper * (1.0 - tangent * tangent) * gelu_scale * (
        1.0 + 3.0 * gelu_cubic * upper * upper
    )
    return (active, slope)


def adamw_update(parameter, gradient, moments, decay_rate):
    first_moment = beta_first * moments[0] + (1.0 - beta_first) * gradient
    second = beta_second * moments[1] + (1.0 - beta_second) * gradient * gradient
    unbiased_first = first_moment / (1.0 - beta_first**adam_steps)
    unbiased_second = second / (1.0 - beta_second**adam_steps)
    update = unbiased_first / (jnp.sqrt(unbiased_second) + adam_epsilon) + decay_rate * parameter
    return (parameter - learn_rate * update, jnp.stack([first_moment, second]))


def collect_columns(piece, groups, inner):
    rows = piece.shape[0] // groups
    parts = piece.reshape(rows * groups, -1, 1, inner)
    moved = lax.all_to_all(parts, "seq", 0, 2, tiled=True)
    return moved.reshape(rows, -1)


def body(
    tokens,
    output_cotangent,
    placement,
    inward,
    outward,
    attend_vectors,
    expand,
    shrink,
    feed_vectors,
    expand_bias,
    inward_moments,
    outward_moments,
    attend_moments,
    expand_moments,
    shrink_moments,
    feed_moments,
    bias_moments,
):
    slot_count, block_size, model_width = tokens.shape
    groups = lax.axis_size("seq")
    replicas = lax.axis_size("dp")
    devices = groups * replicas
    mine = lax.axis_index("seq")
    length = block_size * groups
    row_count = slot_count * block_size
    all_rows = slot_count * length
    head_count = HEADS // groups
    part_width = head_count * HEAD_DIM
    vec_width = attend_vectors.shape[1]
    hidden_part = expand_bias.shape[0]
    score_scale = 1.0 / math.sqrt(HEAD_DIM)

    def gather_rows(local):
        full = lax.all_gather(
            local.reshape(slot_count, block_size, -1), "seq", axis=1, tiled=True
        )
        return full.reshape(all_rows, -1)

    def scatter_rows(partial):
        own = lax.psum_scatter(
            halved(partial).reshape(slot_count, length, -1), "seq", scatter_dimension=1, tiled=True
        )
        return own.reshape(row_count, -1).astype(jnp.float32)

    slot_ids = lax.axis_index("dp") * slot_count + jnp.arange(slot_count, dtype=jnp.int32)
    live_mask = jnp.any(placement[None, :] == slot_ids[:, None], axis=1).astype(jnp.float32)[
        :, None, None
    ]

    small = jnp.concatenate(
        [
            halved(attend_vectors).reshape(-1),
            halved(feed_vectors).reshape(-1),
            halved(expand_bias),
        ]
    )
    small_size = small.shape[0]
    pad_rows = 16
    in_rows = inward.shape[0]
    block_rows = groups * in_rows
    small_row = jnp.broadcast_to(
        jnp.pad(small, (0, model_width - small_size)), (groups, 1, model_width)
    )
    both = jnp.concatenate([halved(inward), halved(outward)], axis=1)
    both_parts = jnp.transpose(both.reshape(in_rows, -1, groups, part_width), (2, 0, 1, 3))
    up_parts = jnp.transpose(
        halved(expand).reshape(in_rows, replicas, groups, hidden_part), (2, 0, 1, 3)
    )
    moved = lax.all_to_all(
        jnp.concatenate(
            [
                both_parts.reshape(groups, in_rows, model_width),
                up_parts.reshape(groups, in_rows, model_width),
                small_row,
            ],
            axis=1,
        ),
        "seq",
        0,
        0,
        tiled=True,
    )
    small_block = jnp.pad(moved[:, 2 * in_rows], ((0, pad_rows - groups), (0, 0)))
    first = lax.all_gather(
        jnp.concatenate(
            [moved[:, :in_rows].reshape(block_rows, model_width), small_block], axis=0
        ),
        "dp",
        axis=0,
        tiled=True,
    ).reshape(replicas, block_rows + pad_rows, model_width)
    both_part = first[:, :block_rows].reshape(model_width, model_width)
    in_part = both_part[:, : 3 * part_width]
    out_part = both_part[:, 3 * part_width :]
    small_all = (
        first[:, block_rows : block_rows + groups, :small_size]
        .reshape(devices, small_size)
        .astype(jnp.float32)
    )
    vectors = jnp.transpose(
        small_all[:, : 8 * vec_width].reshape(devices, 8, vec_width), (1, 0, 2)
    ).reshape(8, model_width)
    vec_one = vectors[:5]
    vec_two = vectors[5:]
    bias_all = small_all[:, 8 * vec_width :].reshape(replicas, groups, hidden_part)
    bias_part = lax.dynamic_index_in_dim(bias_all, mine, 1, keepdims=False).reshape(-1)
    up_part = lax.all_gather(
        moved[:, in_rows : 2 * in_rows].reshape(block_rows, model_width),
        "dp",
        axis=0,
        tiled=True,
    )
    down_part = lax.all_gather(halved(shrink), "dp", axis=0, tiled=True)

    cotangent = (output_cotangent * live_mask).reshape(row_count, model_width)
    cot_all = gather_rows(halved(cotangent))
    feed_bias_grad = jnp.sum(cotangent, axis=0)

    flat_tokens = tokens.reshape(row_count, model_width)
    normed_one, inverse_one = normalize(flat_tokens)
    lifted_one = gather_rows(halved(normed_one * vec_one[0] + vec_one[1]))
    packed = jnp.dot(lifted_one, in_part, preferred_element_type=jnp.float32)
    bias_query = lax.dynamic_slice_in_dim(vec_one[2], mine * part_width, part_width)
    bias_value = lax.dynamic_slice_in_dim(vec_one[3], mine * part_width, part_width)

    def to_heads(operand):
        return jnp.transpose(
            operand.reshape(slot_count, length, head_count, HEAD_DIM), (0, 2, 1, 3)
        )

    def from_heads(operand):
        return jnp.transpose(operand, (0, 2, 1, 3)).reshape(all_rows, part_width)

    queries = to_heads(halved(packed[:, :part_width] + bias_query))
    keys = to_heads(halved(packed[:, part_width : 2 * part_width]))
    values = to_heads(halved(packed[:, 2 * part_width :] + bias_value))
    positions = jnp.arange(length)
    allowed = positions[None, :] <= positions[:, None]
    scores = (
        jnp.einsum("shqd,shkd->shqk", queries, keys, preferred_element_type=jnp.float32)
        * score_scale
    )
    scores = jnp.where(allowed, scores, masked_score)
    score_peak = jnp.max(scores, axis=-1, keepdims=True)
    log_total = score_peak + jnp.log(jnp.sum(jnp.exp(scores - score_peak), axis=-1, keepdims=True))
    weights_full = jnp.exp(scores - log_total)
    weights_half = halved(weights_full)
    attended_heads = halved(
        jnp.einsum("shqk,shkd->shqd", weights_half, values, preferred_element_type=jnp.float32)
    )
    attended = lax.all_gather(from_heads(attended_heads), "seq", axis=0, tiled=False)
    attended = jnp.transpose(attended, (1, 0, 2)).reshape(all_rows, model_width)
    projected = lax.all_to_all(
        halved(jnp.dot(attended, out_part, preferred_element_type=jnp.float32)).reshape(
            slot_count, length, part_width
        ),
        "seq",
        1,
        2,
        tiled=True,
    ).reshape(row_count, model_width)
    middle = flat_tokens + projected + vec_one[4]
    normed_two, inverse_two = normalize(middle)
    lifted_two = gather_rows(halved(normed_two * vec_two[0] + vec_two[1]))
    upper = jnp.dot(lifted_two, up_part, preferred_element_type=jnp.float32) + bias_part
    active_full, slope = gelu_pair(upper)
    active = halved(active_full)
    upper_grad = (
        lax.dot_general(
            cot_all, down_part, (((1,), (1,)), ((), ())), preferred_element_type=jnp.float32
        )
        * slope
    )
    upper_half = halved(upper_grad)
    lift_two_grad = scatter_rows(
        lax.dot_general(
            upper_half, up_part, (((1,), (1,)), ((), ())), preferred_element_type=jnp.float32
        )
    )
    fed = scatter_rows(jnp.dot(active, down_part, preferred_element_type=jnp.float32))
    block_output = (middle + fed + vec_two[2]).reshape(
        slot_count, block_size, model_width
    ) * live_mask

    def outer(left, right):
        return halved(
            lax.dot_general(
                left, right, (((0,), (0,)), ((), ())), preferred_element_type=jnp.float32
            )
        )

    shrink_sum = lax.psum_scatter(
        outer(active, cot_all), "dp", scatter_dimension=0, tiled=True
    ).astype(jnp.float32)
    expand_sum = collect_columns(
        lax.psum_scatter(outer(lifted_two, upper_half), "dp", scatter_dimension=0, tiled=True),
        groups,
        hidden_part,
    ).astype(jnp.float32)
    bias_grad = jnp.sum(upper_grad, axis=0).reshape(replicas, 1, hidden_part)

    gain_two_grad = jnp.sum(lift_two_grad * normed_two, axis=0)
    shift_two_grad = jnp.sum(lift_two_grad, axis=0)
    middle_grad = cotangent + norm_back(lift_two_grad * vec_two[0], normed_two, inverse_two)
    middle_half = halved(middle_grad)
    out_bias_grad = jnp.sum(middle_grad, axis=0)
    middle_cols = lax.all_to_all(
        middle_half.reshape(slot_count, block_size, model_width), "seq", 2, 1, tiled=True
    ).reshape(all_rows, part_width)
    attended_back = halved(
        lax.dot_general(
            middle_cols, out_part, (((1,), (1,)), ((), ())), preferred_element_type=jnp.float32
        )
    )
    attended_grad = to_heads(
        lax.psum_scatter(
            jnp.transpose(attended_back.reshape(all_rows, groups, part_width), (1, 0, 2)),
            "seq",
            scatter_dimension=0,
            tiled=True,
        ).reshape(all_rows, part_width)
    )
    outward_part = outer(attended, middle_cols)
    delta_sum = jnp.sum(
        attended_grad.astype(jnp.float32) * attended_heads.astype(jnp.float32),
        axis=-1,
        keepdims=True,
    )
    weight_grad = jnp.einsum(
        "shqd,shkd->shqk", attended_grad, values, preferred_element_type=jnp.float32
    )
    score_grad = halved(weights_full * (weight_grad - delta_sum) * score_scale)
    query_grad = from_heads(
        jnp.einsum("shqk,shkd->shqd", score_grad, keys, preferred_element_type=jnp.float32)
    )
    key_grad = from_heads(
        jnp.einsum("shqk,shqd->shkd", score_grad, queries, preferred_element_type=jnp.float32)
    )
    value_grad = from_heads(
        jnp.einsum(
            "shqk,shqd->shkd", weights_half, attended_grad, preferred_element_type=jnp.float32
        )
    )
    packed_grad = halved(jnp.concatenate([query_grad, key_grad, value_grad], axis=1))
    lift_one_grad = scatter_rows(
        lax.dot_general(
            packed_grad, in_part, (((1,), (1,)), ((), ())), preferred_element_type=jnp.float32
        )
    )
    inward_part = outer(lifted_one, packed_grad)

    def place_part(part):
        return lax.dynamic_update_slice_in_dim(
            jnp.zeros((model_width,), jnp.float32), part, mine * part_width, 0
        )

    gain_one_grad = jnp.sum(lift_one_grad * normed_one, axis=0)
    shift_one_grad = jnp.sum(lift_one_grad, axis=0)
    tokens_grad = middle_grad + norm_back(lift_one_grad * vec_one[0], normed_one, inverse_one)
    input_gradient = tokens_grad.reshape(slot_count, block_size, model_width) * live_mask
    vector_grads = jnp.stack(
        [
            gain_one_grad,
            shift_one_grad,
            place_part(jnp.sum(query_grad, axis=0)),
            place_part(jnp.sum(value_grad, axis=0)),
            out_bias_grad,
            gain_two_grad,
            shift_two_grad,
            feed_bias_grad,
        ]
    ).reshape(8, devices, vec_width)
    bias_placed = lax.dynamic_update_slice_in_dim(
        jnp.zeros((replicas, groups, hidden_part), jnp.float32), bias_grad, mine, 1
    ).reshape(devices, hidden_part)
    small_grads = halved(
        jnp.concatenate(
            [jnp.transpose(vector_grads, (1, 0, 2)).reshape(devices, 8 * vec_width), bias_placed],
            axis=1,
        )
    ).reshape(replicas, groups, small_size)
    small_grads = jnp.pad(
        small_grads, ((0, 0), (0, pad_rows - groups), (0, model_width - small_size))
    )
    both_grads = jnp.concatenate([inward_part, outward_part], axis=1).reshape(
        replicas, block_rows, model_width
    )
    reduced = lax.psum_scatter(
        jnp.concatenate([both_grads, small_grads], axis=1).reshape(-1, model_width),
        "dp",
        scatter_dimension=0,
        tiled=True,
    )
    returned = lax.all_to_all(
        jnp.concatenate(
            [
                reduced[:block_rows].reshape(groups, in_rows, model_width),
                reduced[block_rows : block_rows + groups].reshape(groups, 1, model_width),
            ],
            axis=1,
        ),
        "seq",
        0,
        0,
        tiled=True,
    )
    both_sum = jnp.transpose(
        returned[:, :in_rows].reshape(groups, in_rows, -1, part_width), (1, 2, 0, 3)
    ).reshape(in_rows, -1).astype(jnp.float32)
    inward_sum = both_sum[:, : 3 * model_width]
    outward_sum = both_sum[:, 3 * model_width :]
    small_sum = jnp.sum(returned[:, in_rows, :small_size].astype(jnp.float32), axis=0)
    vector_sum = small_sum[: 8 * vec_width].reshape(8, vec_width)
    attend_vec_sum = vector_sum[:5]
    feed_vec_sum = vector_sum[5:]
    bias_sum = small_sum[8 * vec_width :]
    inward_new, inward_state = adamw_update(inward, inward_sum, inward_moments, weight_decay)
    outward_new, outward_state = adamw_update(outward, outward_sum, outward_moments, weight_decay)
    attend_new, attend_state = adamw_update(attend_vectors, attend_vec_sum, attend_moments, 0.0)
    expand_new, expand_state = adamw_update(expand, expand_sum, expand_moments, weight_decay)
    shrink_new, shrink_state = adamw_update(shrink, shrink_sum, shrink_moments, weight_decay)
    feed_new, feed_state = adamw_update(feed_vectors, feed_vec_sum, feed_moments, 0.0)
    bias_new, bias_state = adamw_update(expand_bias, bias_sum, bias_moments, 0.0)
    return (
        block_output,
        input_gradient,
        inward_sum,
        outward_sum,
        attend_vec_sum,
        expand_sum,
        shrink_sum,
        feed_vec_sum,
        bias_sum,
        inward_new,
        outward_new,
        attend_new,
        expand_new,
        shrink_new,
        feed_new,
        bias_new,
        inward_state,
        outward_state,
        attend_state,
        expand_state,
        shrink_state,
        feed_state,
        bias_state,
    )


MESH = pl.DeviceIdType.MESH
copy_slots = 160


def mm(left, right):
    return lax.dot_general(
        left, right, (((1,), (0,)), ((), ())), preferred_element_type=jnp.float32
    )


def mm_nt(left, right):
    return lax.dot_general(
        left, right, (((1,), (1,)), ((), ())), preferred_element_type=jnp.float32
    )


def mm_tn(left, right):
    return lax.dot_general(
        left, right, (((0,), (0,)), ((), ())), preferred_element_type=jnp.float32
    )


def wide(operand):
    return operand.astype(jnp.float32)


def scratch_plan(slots, length, block, width, head_count, in_rows, hidden):
    half, full = jnp.bfloat16, jnp.float32
    rows = slots * block
    part = head_count * HEAD_DIM
    dp_rows = in_rows * 4
    pairs = slots * head_count
    return dict(
        s_in=((4, in_rows, 3 * part), half),
        s_up=((4, in_rows, hidden), half),
        in_all=((width, 4 * part), half),
        up_all=((width, hidden), half),
        down_all=((hidden, width), half),
        out_ring=((4, 2, in_rows, width), half),
        out_all=((4, 2, in_rows, width), half),
        live=((rows, 1), full),
        small=((16, 128), full),
        small_land=((4, 8, 128), full),
        small_all=((8, 16, 128), full),
        vecs=((16, width), full),
        normed_one=((rows, width), full),
        inverse_one=((rows, 1), full),
        lifted_one=((slots, length, width), half),
        cot_all=((slots, length, width), half),
        q_h=((pairs, length, HEAD_DIM), half),
        k_h=((pairs, length, HEAD_DIM), half),
        v_h=((pairs, length, HEAD_DIM), half),
        weights=((pairs, length, length), full),
        att_h=((pairs, length, HEAD_DIM), half),
        attended=((slots, length, part), half),
        proj_p=((slots, length, width), half),
        proj_c=((2, slots, block, width), half),
        proj_b=((slots, block, width), half),
        proj_y=((slots, block, width), half),
        middle=((rows, width), full),
        normed_two=((rows, width), full),
        inverse_two=((rows, 1), full),
        lifted_two=((slots, length, width), half),
        active=((slots, length, hidden), half),
        slope=((slots, length, hidden), full),
        upper_half=((slots, length, hidden), half),
        two_p=((slots, length, width), half),
        two_c=((2, slots, block, width), half),
        two_b=((slots, block, width), half),
        two_y=((slots, block, width), half),
        fed_p=((slots, length, width), half),
        fed_c=((2, slots, block, width), half),
        fed_b=((slots, block, width), half),
        fed_y=((slots, block, width), half),
        one_p=((slots, length, width), half),
        one_c=((2, slots, block, width), half),
        one_b=((slots, block, width), half),
        one_y=((slots, block, width), half),
        mid_all=((slots, length, width), half),
        mid_grad=((rows, width), full),
        ag_h=((pairs, length, HEAD_DIM), half),
        pg_h=((3, pairs, length, HEAD_DIM), half),
        bias_h=((2, pairs, 1, HEAD_DIM), full),
        pg=((slots, length, 3 * part), half),
        sh_s=((2, 4, dp_rows, width), half),
        sh_l=((2, 4, dp_rows, width), half),
        ex_s=((2, 4, dp_rows, hidden), half),
        ex_l=((2, 4, dp_rows, hidden), half),
        ex_f=((dp_rows, hidden), half),
        ex_g=((4, in_rows, hidden), half),
        low_s=((2, 4, dp_rows, 2 * part), half),
        low_l=((2, 4, dp_rows, 2 * part), half),
        high_s=((2, 4, dp_rows, 2 * part), half),
        high_l=((2, 4, dp_rows, 2 * part), half),
        in_f=((dp_rows, 3 * part), half),
        in_g=((4, in_rows, 3 * part), half),
        og=((4, 2, in_rows, width), half),
        og_ring=((4, 2, in_rows, width), half),
        g_full=((16, width), full),
        g_out=((2, 4, 16, 128), full),
        g_l=((4, 16, 128), full),
        g_z=((3, 16, 128), full),
        g_f=((8, 128), full),
        g_g=((4, 8, 128), full),
    )


def layer_kernel(names, *refs):
    r = types.SimpleNamespace(**dict(zip(names, refs)))
    ssem, rsem = r.ssem, r.rsem
    slots, length, width = r.lifted_one.shape
    rows = r.middle.shape[0]
    block = rows // slots
    pairs = r.q_h.shape[0]
    heads = pairs // slots
    part = heads * HEAD_DIM
    in_rows = r.outward.shape[0]
    dp_rows = 4 * in_rows
    hidden = r.up_all.shape[1]
    score_scale = 1.0 / math.sqrt(HEAD_DIM)

    dp, me = lax.axis_index("dp"), lax.axis_index("seq")
    z, x = dp // 2, dp % 2
    y, core = me // 2, me % 2
    sib = me + 1 - 2 * core
    yp = (me + 2) % 4
    xdp = dp + 1 - 2 * x
    turn = y + 2 * core

    def z_dp(k):
        return 2 * ((z + k) % 4) + x

    place = (1 - x) * z + x * (7 - z)

    def ring_dp(k):
        at = (place + k + 8) % 8
        return (1 - at // 4) * 2 * at + (at // 4) * (15 - 2 * at)

    right, left = (ring_dp(1), me), (ring_dp(-1), me)

    used = [0]
    sent = []

    def slot():
        used[0] += 1
        return used[0] - 1

    def rc(source, target, device, at=None, start=True):
        index = slot() if at is None else at
        copy = pltpu.make_async_remote_copy(
            source,
            target,
            ssem.at[index],
            rsem.at[index],
            device_id=device,
            device_id_type=MESH,
        )
        if start:
            copy.start()
            if at is None:
                sent.append(copy)
        return copy

    barrier = pltpu.get_barrier_semaphore()
    for device in (
        [(dp, (me + k) % 4) for k in (1, 2, 3)]
        + [(z_dp(k), me) for k in (1, 2, 3)]
        + [(xdp, me)]
    ):
        pl.semaphore_signal(barrier, inc=1, device_id=device, device_id_type=MESH)

    def seq_rows(which):
        return pl.ds(which * block, block)

    class SeqGather:
        def __init__(self, buf):
            self.buf = buf
            own = seq_rows(me)
            self.far = [rc(buf.at[s, own], buf.at[s, own], (dp, yp)) for s in range(slots)]
            self.near = rc(buf.at[:, own], buf.at[:, own], (dp, sib))

        def forward(self):
            theirs = seq_rows(yp)
            self.passed = []
            for s in range(slots):
                self.far[s].wait_recv()
                self.passed.append(
                    rc(self.buf.at[s, theirs], self.buf.at[s, theirs], (dp, sib))
                )

        def finish(self):
            self.near.wait_recv()
            for copy in self.passed:
                copy.wait_recv()

    class SeqScatter:
        def __init__(self, partial, near, sums, far):
            self.p, self.c, self.b, self.y = partial, near, sums, far
            self.base = slot()
            slot()

        def near_copy(self, index, which):
            return rc(
                self.p.at[:, seq_rows(which)],
                self.c.at[1 - index],
                (dp, sib),
                at=self.base + index,
                start=False,
            )

        def order(self, index):
            return (me + (1 - index // 2) * (sib - me) + 2 * (1 - index % 2)) % 4

        def fill(self, compute):
            def step(index, carry):
                which = self.order(index)
                value = compute(which)
                self.p[:, seq_rows(which)] = halved(value).reshape(slots, block, width)

                @pl.when(index < 2)
                def _():
                    self.near_copy(index, which).start()

                return carry

            lax.fori_loop(0, 4, step, 0)
            for index in range(2):
                sent.append(self.near_copy(index, self.order(index)))

        def middle(self):
            self.near_copy(0, self.order(0)).wait_recv()
            self.far = []
            for s in range(slots):
                self.b[s] = halved(wide(self.p[s, seq_rows(yp)]) + wide(self.c[1, s]))
                self.far.append(rc(self.b.at[s], self.y.at[s], (dp, yp)))

        def finish(self):
            self.near_copy(1, self.order(1)).wait_recv()
            for copy in self.far:
                copy.wait_recv()
            total = wide(self.p[:, seq_rows(me)]) + wide(self.c[0]) + wide(self.y[...])
            return total.reshape(rows, width)

    class SmallGather:
        def __init__(self, buf):
            self.buf = buf

        def send(self):
            own = self.buf.at[dp]
            self.far = [rc(own, own, (z_dp(k), me)) for k in (1, 2, 3)]
            self.near = [rc(own, own, (xdp, me))]

        def forward(self):
            for k in (1, 2, 3):
                self.far[k - 1].wait_recv()
                theirs = self.buf.at[z_dp(4 - k)]
                self.near.append(rc(theirs, theirs, (xdp, me)))

        def finish(self):
            for copy in self.near:
                copy.wait_recv()

    half_rows = dp_rows // 2

    class RingGather:
        def __init__(self, buf):
            self.buf, self.moving = buf, []

        def at(self, which, piece=None):
            start = which * dp_rows
            if piece is None:
                return self.buf.at[pl.ds(pl.multiple_of(start, dp_rows), dp_rows)]
            start = start + piece * half_rows
            return self.buf.at[pl.ds(pl.multiple_of(start, half_rows), half_rows)]

        def step(self, j):
            self.finish()
            ahead = self.at(ring_dp(1 - j), 0 if j == 4 else None)
            back = self.at(ring_dp(j - 1), 1 if j == 4 else None)
            self.moving = [rc(ahead, ahead, right), rc(back, back, left)]

        def finish(self):
            for copy in self.moving:
                copy.wait_recv()

    class RingScatter:
        def __init__(self, chunk, away, land):
            self.chunk, self.away, self.land, self.moving = chunk, away, land, []

        def arrive(self):
            for copy in self.moving:
                copy.wait_recv()

        def step(self, j):
            if j == 1:
                value = halved(self.chunk(ring_dp(4)))
                here = slice(0, half_rows)
                self.away[0, 0, here] = value[:half_rows]
                self.away[1, 0, here] = value[half_rows:]
                rows_sent = pl.ds(0, half_rows)
            else:
                ahead, back = self.chunk(ring_dp(5 - j)), self.chunk(ring_dp(j - 5))
                self.arrive()
                if j == 2:
                    near = wide(self.land[0, 0, 0:half_rows])
                    far = wide(self.land[1, 0, 0:half_rows])
                    self.away[0, 1, 0:half_rows] = halved(ahead[:half_rows] + near)
                    self.away[0, 1, half_rows:dp_rows] = halved(ahead[half_rows:])
                    self.away[1, 1, 0:half_rows] = halved(back[:half_rows])
                    self.away[1, 1, half_rows:dp_rows] = halved(back[half_rows:] + far)
                else:
                    self.away[0, j - 1] = halved(ahead + wide(self.land[0, j - 2]))
                    self.away[1, j - 1] = halved(back + wide(self.land[1, j - 2]))
                rows_sent = pl.ds(0, dp_rows)
            self.moving = [
                rc(
                    self.away.at[way, j - 1, rows_sent],
                    self.land.at[way, j - 1, rows_sent],
                    target,
                )
                for way, target in ((0, right), (1, left))
            ]

        def finish(self):
            own = self.chunk(dp)
            self.arrive()
            return own + (wide(self.land[0, 3]) + wide(self.land[1, 3]))

    def chunk_of(left_ref, right_ref):
        def chunk(which):
            at = pl.ds(pl.multiple_of(which * dp_rows, dp_rows), dp_rows)
            return mm_tn(
                left_ref[:, :, at].reshape(-1, dp_rows), right_ref[...].reshape(slots * length, -1)
            )

        return chunk

    vec_width = r.attend_vectors.shape[1]
    r.small[0:5, 0:vec_width] = r.attend_vectors[...]
    r.small[5:8, 0:vec_width] = r.feed_vectors[...]
    spread = jnp.concatenate([r.small[0:8, 0:vec_width]] * 4, axis=1)
    lane = lax.broadcasted_iota(jnp.int32, spread.shape, 1)
    r.small[0:8] = wide(halved(jnp.where(lane // vec_width == me, spread, 0.0)))
    r.small[8:16] = jnp.broadcast_to(wide(halved(r.expand_bias[...])), (8, 128))
    for s in range(slots):
        found = jnp.int32(0)
        for i in range(r.placement.shape[0]):
            found = jnp.where(r.placement[i] == dp * slots + s, 1, found)
        r.live[s * block : (s + 1) * block] = jnp.full((block, 1), found.astype(jnp.float32))

    dp_at = pl.ds(pl.multiple_of(dp * dp_rows, dp_rows), dp_rows)
    own_at = pl.ds(pl.multiple_of(dp * dp_rows + me * in_rows, in_rows), in_rows)
    r.down_all[dp_at] = halved(r.shrink[...])
    r.small_land[0] = r.small[0:8]
    down, inward, up = RingGather(r.down_all), RingGather(r.in_all), RingGather(r.up_all)
    pl.semaphore_wait(barrier, 7)
    down.step(1)
    small_seq = [
        rc(r.small_land.at[0], r.small_land.at[k], (dp, (me + k) % 4)) for k in (1, 2, 3)
    ]

    for g in range(4):
        turn_g = g // 2 + 2 * (g % 2)
        for third in range(3):
            pieces = [
                r.inward[:, pl.ds(third * width + (4 * j + turn_g) * HEAD_DIM, HEAD_DIM)]
                for j in range(heads)
            ]
            r.s_in[g, :, third * part : (third + 1) * part] = halved(
                jnp.concatenate(pieces, axis=1)
            )
    in_at = r.in_all.at[own_at, pl.ds(0, 3 * part)]
    in_seq = [
        rc(r.s_in.at[(me + k) % 4], in_at, (dp, (me + k) % 4)) for k in (2, 3, 1)
    ]
    in_at[...] = r.s_in[me]
    for i in range(4):
        rows_at = pl.ds(pl.multiple_of(dp * dp_rows + i * in_rows, in_rows), in_rows)
        r.in_all[rows_at, 3 * part : 4 * part] = halved(r.outward[:, i * part : (i + 1) * part])
    for g in range(4):
        for d in range(hidden // 128):
            r.s_up[g, :, d * 128 : (d + 1) * 128] = halved(
                r.expand[:, pl.ds((d * 4 + g) * 128, 128)]
            )
    up_seq = [
        rc(r.s_up.at[(me + k) % 4], r.up_all.at[own_at], (dp, (me + k) % 4))
        for k in (2, 3, 1)
    ]
    r.up_all[own_at] = r.s_up[me]

    normed, inverse = normalize(r.tokens[...])
    r.normed_one[...] = normed
    r.inverse_one[...] = inverse
    cotangent = r.cot[...] * r.live[...]
    r.cot_all[:, seq_rows(me)] = halved(cotangent).reshape(slots, block, width)

    for copy in small_seq:
        copy.wait_recv()
    mine_small = r.small_all.at[dp]
    mine_small[0:8] = (r.small_land[0] + r.small_land[1]) + (
        r.small_land[2] + r.small_land[3]
    )
    mine_small[8:16] = r.small[8:16]
    small = SmallGather(r.small_all)
    small.send()

    for copy in in_seq:
        copy.wait_recv()
    inward.step(1)
    small.forward()
    inward.step(2)
    down.step(2)
    small.finish()
    for d in range(8):
        r.vecs[:, d * 128 : (d + 1) * 128] = r.small_all[d]

    def vec(index):
        return r.vecs[index : index + 1, :]

    r.lifted_one[:, seq_rows(me)] = halved(
        r.normed_one[...] * vec(0) + vec(1)
    ).reshape(slots, block, width)
    lift_one = SeqGather(r.lifted_one)

    inward.step(3)
    down.step(3)
    lift_one.forward()
    cot = SeqGather(r.cot_all)
    inward.step(4)
    for copy in up_seq:
        copy.wait_recv()
    up.step(1)
    cot.forward()
    down.step(4)
    lift_one.finish()
    inward.finish()
    up.step(2)
    for d in range(8):
        r.out_ring[d // 2, d % 2] = jnp.concatenate(
            [
                r.in_all[d * dp_rows + i * in_rows : d * dp_rows + (i + 1) * in_rows, 3 * part :]
                for i in range(4)
            ],
            axis=1,
        )
    r.out_all[:, core] = r.out_ring[:, core]
    out_pair = rc(r.out_ring.at[:, 1 - core], r.out_all.at[:, core], (dp, sib))

    def own_heads(row):
        pieces = []
        for j in range(heads):
            piece = jnp.zeros((1, HEAD_DIM), jnp.float32)
            for t in range(4):
                start = (4 * j + t) * HEAD_DIM
                piece = jnp.where(turn == t, row[:, start : start + HEAD_DIM], piece)
            pieces.append(piece)
        return jnp.concatenate(pieces, axis=1)

    bias_query, bias_value = own_heads(vec(2)), own_heads(vec(3))

    def project_in(s, carry):
        packed = mm(r.lifted_one[s], r.in_all[:, : 3 * part])
        queries = halved(packed[:, :part] + bias_query)
        keys = halved(packed[:, part : 2 * part])
        values = halved(packed[:, 2 * part :] + bias_value)
        for j in range(heads):
            cut = slice(j * HEAD_DIM, (j + 1) * HEAD_DIM)
            r.q_h[s * heads + j] = queries[:, cut]
            r.k_h[s * heads + j] = keys[:, cut]
            r.v_h[s * heads + j] = values[:, cut]
        return carry

    lax.fori_loop(0, slots, project_in, 0)

    def attend(p, carry):
        scores = mm_nt(r.q_h[p], r.k_h[p]) * score_scale
        row_at = lax.broadcasted_iota(jnp.int32, scores.shape, 0)
        column_at = lax.broadcasted_iota(jnp.int32, scores.shape, 1)
        scores = jnp.where(column_at <= row_at, scores, masked_score)
        peak = jnp.max(scores, axis=-1, keepdims=True)
        raised = jnp.exp(scores - peak)
        weights = raised * (1.0 / jnp.sum(raised, axis=-1, keepdims=True))
        r.weights[p] = weights
        r.att_h[p] = halved(mm(halved(weights), r.v_h[p]))
        return carry

    lax.fori_loop(0, pairs, attend, 0)
    for s in range(slots):
        r.attended[s] = jnp.concatenate(
            [r.att_h[s * heads + j] for j in range(heads)], axis=1
        )

    up.step(3)
    out_pair.wait_recv()
    proj = SeqScatter(r.proj_p, r.proj_c, r.proj_b, r.proj_y)
    proj.fill(
        lambda which: mm(
            r.attended[:, seq_rows(which)].reshape(rows, part), r.out_all[...].reshape(part, width)
        )
    )
    proj.middle()
    up.step(4)
    middle = r.tokens[...] + proj.finish() + vec(4)
    r.middle[...] = middle
    normed, inverse = normalize(middle)
    r.normed_two[...] = normed
    r.inverse_two[...] = inverse
    r.lifted_two[:, seq_rows(me)] = halved(normed * vec(5) + vec(6)).reshape(
        slots, block, width
    )
    lift_two = SeqGather(r.lifted_two)
    lift_two.forward()
    lift_two.finish()
    cot.finish()
    up.finish()

    def feed(index, carry):
        here = seq_rows(index)
        upper = mm(r.lifted_two[:, here].reshape(rows, width), r.up_all[...]) + vec(8)
        active, slope = gelu_pair(upper)
        r.active[:, here] = halved(active).reshape(slots, block, hidden)
        r.slope[:, here] = slope.reshape(slots, block, hidden)
        return carry

    lax.fori_loop(0, 4, feed, 0)
    shrink = RingScatter(chunk_of(r.active, r.cot_all), r.sh_s, r.sh_l)
    shrink.step(1)
    down.finish()

    two = SeqScatter(r.two_p, r.two_c, r.two_b, r.two_y)
    r.g_full[8:9, :] = jnp.zeros((1, hidden), jnp.float32)

    def feed_back(which):
        here = seq_rows(which)
        upper_grad = mm_nt(
            r.cot_all[:, here].reshape(rows, width), r.down_all[...]
        ) * r.slope[:, here].reshape(rows, hidden)
        r.g_full[8:9, :] += jnp.sum(upper_grad, axis=0, keepdims=True)
        upper_half = halved(upper_grad)
        r.upper_half[:, here] = upper_half.reshape(slots, block, hidden)
        return mm_nt(upper_half, r.up_all[...])

    two.fill(feed_back)
    two.middle()
    expand = RingScatter(chunk_of(r.lifted_two, r.upper_half), r.ex_s, r.ex_l)
    expand.step(1)
    shrink.step(2)
    fed = SeqScatter(r.fed_p, r.fed_c, r.fed_b, r.fed_y)
    fed.fill(
        lambda which: mm(r.active[:, seq_rows(which)].reshape(rows, hidden), r.down_all[...])
    )
    expand.step(2)
    lift_grad = two.finish()
    normed = r.normed_two[...]
    r.g_full[5:6, :] = jnp.sum(lift_grad * normed, axis=0, keepdims=True)
    r.g_full[6:7, :] = jnp.sum(lift_grad, axis=0, keepdims=True)
    cotangent = r.cot[...] * r.live[...]
    r.g_full[7:8, :] = jnp.sum(cotangent, axis=0, keepdims=True)
    middle_grad = cotangent + norm_back(lift_grad * vec(5), normed, r.inverse_two[...])
    r.mid_grad[...] = middle_grad
    r.g_full[4:5, :] = jnp.sum(middle_grad, axis=0, keepdims=True)
    r.mid_all[:, seq_rows(me)] = halved(middle_grad).reshape(slots, block, width)
    mid = SeqGather(r.mid_all)
    shrink.step(3)
    mid.forward()
    fed.middle()
    expand.step(3)
    mid.finish()

    for s in range(slots):
        grads = halved(mm_nt(r.mid_all[s], r.out_all[...].reshape(part, width)))
        for j in range(heads):
            r.ag_h[s * heads + j] = grads[:, j * HEAD_DIM : (j + 1) * HEAD_DIM]

    r.og[...] = halved(
        mm_tn(
            r.attended[...].reshape(slots * length, part),
            r.mid_all[...].reshape(slots * length, width),
        )
    ).reshape(4, 2, in_rows, width)
    r.og_ring[:, core] = r.og[:, core]
    og_pair = rc(r.og.at[:, 1 - core], r.og_ring.at[:, core], (dp, sib))
    shrink.step(4)

    def attend_back(p, carry):
        weights, grads = r.weights[p], r.ag_h[p]
        delta = jnp.sum(wide(grads) * wide(r.att_h[p]), axis=-1, keepdims=True)
        weight_grad = mm_nt(grads, r.v_h[p])
        score_grad = halved(weights * (weight_grad - delta) * score_scale)
        query_grad = mm(score_grad, r.k_h[p])
        key_grad = mm_tn(score_grad, r.q_h[p])
        value_grad = mm_tn(halved(weights), grads)
        r.bias_h[0, p] = jnp.sum(query_grad, axis=0, keepdims=True)
        r.bias_h[1, p] = jnp.sum(value_grad, axis=0, keepdims=True)
        r.pg_h[0, p] = halved(query_grad)
        r.pg_h[1, p] = halved(key_grad)
        r.pg_h[2, p] = halved(value_grad)
        return carry

    lax.fori_loop(0, pairs, attend_back, 0)
    for s in range(slots):
        r.pg[s] = jnp.concatenate(
            [r.pg_h[i, s * heads + j] for i in range(3) for j in range(heads)], axis=1
        )
    expand.step(4)
    og_pair.wait_recv()

    half_width = 2 * part

    def low_chunk(which):
        return chunk_of(r.lifted_one, r.pg.at[:, :, 0:half_width])(which)

    def high_chunk(which):
        ours = r.og_ring[which // 2, which % 2]
        packed = jnp.concatenate(
            [ours[:, i * part : (i + 1) * part] for i in range(4)], axis=0
        )
        last = chunk_of(r.lifted_one, r.pg.at[:, :, half_width : 3 * part])(which)
        return jnp.concatenate([last, wide(packed)], axis=1)

    low = RingScatter(low_chunk, r.low_s, r.low_l)
    high = RingScatter(high_chunk, r.high_s, r.high_l)
    low.step(1)
    high.step(1)
    one = SeqScatter(r.one_p, r.one_c, r.one_b, r.one_y)
    one.fill(
        lambda which: mm_nt(
            r.pg[:, seq_rows(which)].reshape(rows, 3 * part), r.in_all[:, : 3 * part]
        )
    )
    one.middle()
    low.step(2)
    high.step(2)

    block_output = r.middle[...] + fed.finish() + vec(7)
    r.block_output[...] = block_output * r.live[...]
    r.shrink_sum[...] = shrink.finish()
    lift_grad = one.finish()
    normed = r.normed_one[...]
    r.g_full[0:1, :] = jnp.sum(lift_grad * normed, axis=0, keepdims=True)
    r.g_full[1:2, :] = jnp.sum(lift_grad, axis=0, keepdims=True)
    input_gradient = r.mid_grad[...] + norm_back(
        lift_grad * vec(0), normed, r.inverse_one[...]
    )
    r.input_gradient[...] = input_gradient * r.live[...]
    for i in range(2):
        pieces = []
        for head in range(4 * heads):
            total = jnp.zeros((1, HEAD_DIM), jnp.float32)
            for s in range(slots):
                total = total + r.bias_h[i, s * heads + head // 4]
            pieces.append(jnp.where(turn == head % 4, total, 0.0))
        r.g_full[2 + i : 3 + i, :] = jnp.concatenate(pieces, axis=1)
    r.g_full[9:16, :] = jnp.zeros((7, width), jnp.float32)
    for d in range(8):
        r.g_out[d % 2, d // 2] = r.g_full[:, d * 128 : (d + 1) * 128]
    g_near = rc(r.g_out.at[1 - x], r.g_l, (xdp, me))

    low.step(3)
    high.step(3)
    g_near.wait_recv()
    r.g_l[...] = r.g_l[...] + r.g_out[x]
    g_far = [rc(r.g_l.at[(z + k) % 4], r.g_z.at[k - 1], (z_dp(k), me)) for k in (1, 2, 3)]

    r.ex_f[...] = halved(expand.finish())

    def sub(buf, which):
        return buf.at[pl.ds(pl.multiple_of(which * in_rows, in_rows), in_rows)]

    def seq_return(buf, land):
        land[0] = buf[pl.ds(pl.multiple_of(me * in_rows, in_rows), in_rows)]
        return [
            rc(sub(buf, (me + k) % 4), land.at[k], (dp, (me + k) % 4)) for k in (2, 3, 1)
        ]

    ex_back = seq_return(r.ex_f, r.ex_g)
    low.step(4)
    high.step(4)
    for copy in g_far:
        copy.wait_recv()
    g_total = r.g_l[z] + r.g_z[0] + r.g_z[1] + r.g_z[2]
    r.g_f[...] = g_total[0:8]
    r.g_g[0] = g_total[0:8]
    g_back = [rc(r.g_f, r.g_g.at[k], (dp, (me + k) % 4)) for k in (1, 2, 3)]

    for copy in ex_back:
        copy.wait_recv()
    for k in range(4):
        for g in range(4):

            @pl.when((me - k + 4) % 4 == g)
            def _():
                value = wide(r.ex_g[k])
                for d in range(hidden // 128):
                    start = (d * 4 + g) * 128
                    r.expand_sum[:, start : start + 128] = value[:, d * 128 : (d + 1) * 128]

    r.in_f[:, :half_width] = halved(low.finish())
    high_sum = high.finish()
    r.in_f[:, half_width:] = halved(high_sum[:, :part])
    for i in range(4):
        r.outward_sum[:, i * part : (i + 1) * part] = high_sum[
            i * in_rows : (i + 1) * in_rows, part:
        ]
    in_back = seq_return(r.in_f, r.in_g)
    for copy in g_back:
        copy.wait_recv()
    vector_total = (r.g_g[0] + r.g_g[1]) + (r.g_g[2] + r.g_g[3])
    vector_own = jnp.zeros((8, vec_width), jnp.float32)
    for g in range(4):
        vector_own = jnp.where(
            me == g, vector_total[:, g * vec_width : (g + 1) * vec_width], vector_own
        )
    r.attend_sum[...] = vector_own[0:5]
    r.feed_sum[...] = vector_own[5:8]
    r.bias_sum[...] = g_total[8:9]
    for copy in in_back:
        copy.wait_recv()
    by_seq = []
    for g in range(4):
        by_seq.append(r.in_g[(me - g + 4) % 4])
    for third in range(3):
        pieces = []
        for head in range(4 * heads):
            g = 2 * (head % 2) + (head // 2) % 2
            start = third * part + (head // 4) * HEAD_DIM
            pieces.append(by_seq[g][:, start : start + HEAD_DIM])
        r.inward_sum[:, third * width : (third + 1) * width] = wide(
            jnp.concatenate(pieces, axis=1)
        )

    for copy in sent:
        copy.wait_send()


def adamw_kernel(decays, count, *refs):
    kinds = len(decays)
    masters, sums, moments = refs[:kinds], refs[kinds : 2 * kinds], refs[2 * kinds : 3 * kinds]
    passed = refs[3 * kinds : 3 * kinds + count]
    outs = refs[3 * kinds + count :]
    for i, decay in enumerate(decays):
        gradient = sums[i][...]
        fresh, state = outs[kinds + i], outs[2 * kinds + i]
        parameter = masters[i][...]
        turned = moments[i].shape[0] == gradient.shape[0]
        if turned:
            old_first, old_second = moments[i][:, 0], moments[i][:, 1]
        else:
            old_first, old_second = moments[i][0], moments[i][1]
        first_moment = beta_first * old_first + (1.0 - beta_first) * gradient
        second = beta_second * old_second + (1.0 - beta_second) * gradient * gradient
        unbiased_first = first_moment * (1.0 / (1.0 - beta_first**adam_steps))
        unbiased_second = second * (1.0 / (1.0 - beta_second**adam_steps))
        update = unbiased_first / (jnp.sqrt(unbiased_second) + adam_epsilon)
        fresh[...] = parameter - learn_rate * (update + decay * parameter)
        if turned:
            state[:, 0] = first_moment
            state[:, 1] = second
        else:
            state[0] = first_moment
            state[1] = second
        outs[i][...] = gradient
    for i in range(count):
        outs[3 * kinds + i][...] = passed[i][...]


def adamw_call(masters, sums, moments, decays, passed, steps):
    def spec(array):
        axis = array.ndim - 2
        small = array.shape[axis] % (8 * steps) != 0
        block = list(array.shape)
        if not small:
            block[axis] //= steps

        def index(i):
            place = [0] * array.ndim
            if not small:
                place[axis] = i
            return tuple(place)

        return pl.BlockSpec(tuple(block), index)

    arrays = [*masters, *sums, *moments, *passed]
    results = [*sums, *masters, *moments, *passed]
    return pl.pallas_call(
        functools.partial(adamw_kernel, decays, len(passed)),
        grid=(steps,),
        out_shape=[jax.ShapeDtypeStruct(array.shape, jnp.float32) for array in results],
        in_specs=[spec(array) for array in arrays],
        out_specs=[spec(array) for array in results],
        compiler_params=pltpu.CompilerParams(vmem_limit_bytes=60 * 2**20),
        name="adamw",
    )(*arrays)


def fast_body(
    tokens,
    output_cotangent,
    placement,
    inward,
    outward,
    attend_vectors,
    expand,
    shrink,
    feed_vectors,
    expand_bias,
    *moments,
):
    slot_count, block_size, model_width = tokens.shape
    groups = lax.axis_size("seq")
    row_count = slot_count * block_size
    hidden_part = expand.shape[1] // groups
    in_rows = inward.shape[0]

    plan = scratch_plan(
        slot_count,
        block_size * groups,
        block_size,
        model_width,
        HEADS // groups,
        in_rows,
        hidden_part,
    )
    inputs = dict(
        tokens=tokens.reshape(row_count, model_width),
        cot=output_cotangent.reshape(row_count, model_width),
        placement=placement,
        attend_vectors=attend_vectors,
        feed_vectors=feed_vectors,
        expand_bias=expand_bias.reshape(1, -1),
        inward=inward,
        outward=outward,
        expand=expand,
        shrink=shrink,
    )
    outputs = dict(
        block_output=(row_count, model_width),
        input_gradient=(row_count, model_width),
        inward_sum=inward.shape,
        outward_sum=outward.shape,
        expand_sum=expand.shape,
        shrink_sum=shrink.shape,
        attend_sum=attend_vectors.shape,
        feed_sum=feed_vectors.shape,
        bias_sum=(1, expand_bias.shape[0]),
    )
    names = list(inputs) + list(outputs) + list(plan) + ["ssem", "rsem"]
    found = pl.pallas_call(
        functools.partial(layer_kernel, names),
        out_shape=[jax.ShapeDtypeStruct(shape, jnp.float32) for shape in outputs.values()],
        in_specs=[
            pl.BlockSpec(memory_space=pltpu.SMEM if name == "placement" else pltpu.VMEM)
            for name in inputs
        ],
        out_specs=[pl.BlockSpec(memory_space=pltpu.VMEM)] * len(outputs),
        scratch_shapes=[pltpu.VMEM(shape, kind) for shape, kind in plan.values()]
        + [pltpu.SemaphoreType.DMA((copy_slots,)), pltpu.SemaphoreType.DMA((copy_slots,))],
        compiler_params=pltpu.CompilerParams(
            collective_id=0, has_side_effects=True, vmem_limit_bytes=60 * 2**20
        ),
        name="layer",
    )(*inputs.values())
    found = types.SimpleNamespace(**dict(zip(outputs, found)))
    sums = (
        found.inward_sum,
        found.outward_sum,
        found.attend_sum,
        found.expand_sum,
        found.shrink_sum,
        found.feed_sum,
        found.bias_sum,
    )
    masters = (
        inward,
        outward,
        attend_vectors,
        expand,
        shrink,
        feed_vectors,
        expand_bias.reshape(1, -1),
    )
    decays = (weight_decay, weight_decay, 0.0, weight_decay, weight_decay, 0.0, 0.0)

    def turned(index, moment):
        if index in (2, 5):
            return jnp.swapaxes(moment, 0, 1)
        return moment.reshape(moment.shape[:1] + masters[index].shape)

    done = list(adamw_call(
        masters,
        sums,
        [turned(index, moment) for index, moment in enumerate(moments)],
        decays,
        (found.block_output, found.input_gradient),
        2,
    ))
    kinds = len(masters)
    for index in (2, 5):
        done[2 * kinds + index] = jnp.swapaxes(done[2 * kinds + index], 0, 1)
    plain = [*masters[: kinds - 1], expand_bias]
    wanted = [*plain, *plain, *moments, tokens, tokens]
    done = [array.reshape(other.shape) for array, other in zip(done, wanted)]
    return (*done[3 * kinds :], *done[: 3 * kinds])


def solution(mesh):
    chosen = fast_body if (mesh.shape["dp"], mesh.shape["seq"]) == (8, 4) else body
    placed = (
        P("dp", "seq", None),
        P("dp", "seq", None),
        P(),
        P(("dp", "seq"), None),
        P(("dp", "seq"), None),
        P(None, ("dp", "seq")),
        P(("dp", "seq"), None),
        P(("dp", "seq"), None),
        P(None, ("dp", "seq")),
        P(("dp", "seq")),
        P(None, ("dp", "seq"), None),
        P(None, ("dp", "seq"), None),
        P(None, None, ("dp", "seq")),
        P(None, ("dp", "seq"), None),
        P(None, ("dp", "seq"), None),
        P(None, None, ("dp", "seq")),
        P(None, ("dp", "seq")),
    )
    return jax.shard_map(
        chosen,
        mesh=mesh,
        in_specs=placed,
        out_specs=(
            P("dp", "seq", None),
            P("dp", "seq", None),
            P(("dp", "seq"), None),
            P(("dp", "seq"), None),
            P(None, ("dp", "seq")),
            P(("dp", "seq"), None),
            P(("dp", "seq"), None),
            P(None, ("dp", "seq")),
            P(("dp", "seq")),
            P(("dp", "seq"), None),
            P(("dp", "seq"), None),
            P(None, ("dp", "seq")),
            P(("dp", "seq"), None),
            P(("dp", "seq"), None),
            P(None, ("dp", "seq")),
            P(("dp", "seq")),
            P(None, ("dp", "seq"), None),
            P(None, ("dp", "seq"), None),
            P(None, None, ("dp", "seq")),
            P(None, ("dp", "seq"), None),
            P(None, ("dp", "seq"), None),
            P(None, None, ("dp", "seq")),
            P(None, ("dp", "seq")),
        ),
        check_vma=False,
    )
```

```python
import functools
import math
import types

import jax
import jax.numpy as jnp
from jax import lax
from jax.experimental import pallas as pl
from jax.experimental.pallas import tpu as pltpu
from jax.sharding import PartitionSpec as P

HEADS = 16
HEAD_DIM = 64


norm_epsilon = 1e-05
beta_first = 0.9
beta_second = 0.95
adam_epsilon = 1e-08
learn_rate = 0.01
weight_decay = 0.1
adam_steps = 4
gelu_scale = 0.7978845608028654
gelu_cubic = 0.044715
masked_score = -1e30


def halved(operand):
    return operand.astype(jnp.bfloat16)


def normalize(operand):
    average = jnp.mean(operand, axis=-1, keepdims=True)
    centered = operand - average
    variance = jnp.mean(centered * centered, axis=-1, keepdims=True)
    inverse = lax.rsqrt(variance + norm_epsilon)
    return (centered * inverse, inverse)


def norm_back(upstream, normed, inverse):
    first_mean = jnp.mean(upstream, axis=-1, keepdims=True)
    second_mean = jnp.mean(upstream * normed, axis=-1, keepdims=True)
    return inverse * (upstream - first_mean - normed * second_mean)


def gelu_pair(upper):
    inner_arg = gelu_scale * (upper + gelu_cubic * upper * upper * upper)
    tangent = jnp.tanh(inner_arg)
    active = 0.5 * upper * (1.0 + tangent)
    slope = 0.5 * (1.0 + tangent) + 0.5 * upper * (1.0 - tangent * tangent) * gelu_scale * (
        1.0 + 3.0 * gelu_cubic * upper * upper
    )
    return (active, slope)


def adamw_update(parameter, gradient, moments, decay_rate):
    first_moment = beta_first * moments[0] + (1.0 - beta_first) * gradient
    second = beta_second * moments[1] + (1.0 - beta_second) * gradient * gradient
    unbiased_first = first_moment / (1.0 - beta_first**adam_steps)
    unbiased_second = second / (1.0 - beta_second**adam_steps)
    update = unbiased_first / (jnp.sqrt(unbiased_second) + adam_epsilon) + decay_rate * parameter
    return (parameter - learn_rate * update, jnp.stack([first_moment, second]))


def collect_columns(piece, groups, inner):
    rows = piece.shape[0] // groups
    parts = piece.reshape(rows * groups, -1, 1, inner)
    moved = lax.all_to_all(parts, "seq", 0, 2, tiled=True)
    return moved.reshape(rows, -1)


def body(
    tokens,
    output_cotangent,
    placement,
    inward,
    outward,
    attend_vectors,
    expand,
    shrink,
    feed_vectors,
    expand_bias,
    inward_moments,
    outward_moments,
    attend_moments,
    expand_moments,
    shrink_moments,
    feed_moments,
    bias_moments,
):
    slot_count, block_size, model_width = tokens.shape
    groups = lax.axis_size("seq")
    replicas = lax.axis_size("dp")
    devices = groups * replicas
    mine = lax.axis_index("seq")
    length = block_size * groups
    row_count = slot_count * block_size
    all_rows = slot_count * length
    head_count = HEADS // groups
    part_width = head_count * HEAD_DIM
    vec_width = attend_vectors.shape[1]
    hidden_part = expand_bias.shape[0]
    score_scale = 1.0 / math.sqrt(HEAD_DIM)

    def gather_rows(local):
        full = lax.all_gather(
            local.reshape(slot_count, block_size, -1), "seq", axis=1, tiled=True
        )
        return full.reshape(all_rows, -1)

    def scatter_rows(partial):
        own = lax.psum_scatter(
            halved(partial).reshape(slot_count, length, -1), "seq", scatter_dimension=1, tiled=True
        )
        return own.reshape(row_count, -1).astype(jnp.float32)

    slot_ids = lax.axis_index("dp") * slot_count + jnp.arange(slot_count, dtype=jnp.int32)
    live_mask = jnp.any(placement[None, :] == slot_ids[:, None], axis=1).astype(jnp.float32)[
        :, None, None
    ]

    small = jnp.concatenate(
        [
            halved(attend_vectors).reshape(-1),
            halved(feed_vectors).reshape(-1),
            halved(expand_bias),
        ]
    )
    small_size = small.shape[0]
    pad_rows = 16
    in_rows = inward.shape[0]
    block_rows = groups * in_rows
    small_row = jnp.broadcast_to(
        jnp.pad(small, (0, model_width - small_size)), (groups, 1, model_width)
    )
    both = jnp.concatenate([halved(inward), halved(outward)], axis=1)
    both_parts = jnp.transpose(both.reshape(in_rows, -1, groups, part_width), (2, 0, 1, 3))
    up_parts = jnp.transpose(
        halved(expand).reshape(in_rows, replicas, groups, hidden_part), (2, 0, 1, 3)
    )
    moved = lax.all_to_all(
        jnp.concatenate(
            [
                both_parts.reshape(groups, in_rows, model_width),
                up_parts.reshape(groups, in_rows, model_width),
                small_row,
            ],
            axis=1,
        ),
        "seq",
        0,
        0,
        tiled=True,
    )
    small_block = jnp.pad(moved[:, 2 * in_rows], ((0, pad_rows - groups), (0, 0)))
    first = lax.all_gather(
        jnp.concatenate(
            [moved[:, :in_rows].reshape(block_rows, model_width), small_block], axis=0
        ),
        "dp",
        axis=0,
        tiled=True,
    ).reshape(replicas, block_rows + pad_rows, model_width)
    both_part = first[:, :block_rows].reshape(model_width, model_width)
    in_part = both_part[:, : 3 * part_width]
    out_part = both_part[:, 3 * part_width :]
    small_all = (
        first[:, block_rows : block_rows + groups, :small_size]
        .reshape(devices, small_size)
        .astype(jnp.float32)
    )
    vectors = jnp.transpose(
        small_all[:, : 8 * vec_width].reshape(devices, 8, vec_width), (1, 0, 2)
    ).reshape(8, model_width)
    vec_one = vectors[:5]
    vec_two = vectors[5:]
    bias_all = small_all[:, 8 * vec_width :].reshape(replicas, groups, hidden_part)
    bias_part = lax.dynamic_index_in_dim(bias_all, mine, 1, keepdims=False).reshape(-1)
    up_part = lax.all_gather(
        moved[:, in_rows : 2 * in_rows].reshape(block_rows, model_width),
        "dp",
        axis=0,
        tiled=True,
    )
    down_part = lax.all_gather(halved(shrink), "dp", axis=0, tiled=True)

    cotangent = (output_cotangent * live_mask).reshape(row_count, model_width)
    cot_all = gather_rows(halved(cotangent))
    feed_bias_grad = jnp.sum(cotangent, axis=0)

    flat_tokens = tokens.reshape(row_count, model_width)
    normed_one, inverse_one = normalize(flat_tokens)
    lifted_one = gather_rows(halved(normed_one * vec_one[0] + vec_one[1]))
    packed = jnp.dot(lifted_one, in_part, preferred_element_type=jnp.float32)
    bias_query = lax.dynamic_slice_in_dim(vec_one[2], mine * part_width, part_width)
    bias_value = lax.dynamic_slice_in_dim(vec_one[3], mine * part_width, part_width)

    def to_heads(operand):
        return jnp.transpose(
            operand.reshape(slot_count, length, head_count, HEAD_DIM), (0, 2, 1, 3)
        )

    def from_heads(operand):
        return jnp.transpose(operand, (0, 2, 1, 3)).reshape(all_rows, part_width)

    queries = to_heads(halved(packed[:, :part_width] + bias_query))
    keys = to_heads(halved(packed[:, part_width : 2 * part_width]))
    values = to_heads(halved(packed[:, 2 * part_width :] + bias_value))
    positions = jnp.arange(length)
    allowed = positions[None, :] <= positions[:, None]
    scores = (
        jnp.einsum("shqd,shkd->shqk", queries, keys, preferred_element_type=jnp.float32)
        * score_scale
    )
    scores = jnp.where(allowed, scores, masked_score)
    score_peak = jnp.max(scores, axis=-1, keepdims=True)
    log_total = score_peak + jnp.log(jnp.sum(jnp.exp(scores - score_peak), axis=-1, keepdims=True))
    weights_full = jnp.exp(scores - log_total)
    weights_half = halved(weights_full)
    attended_heads = halved(
        jnp.einsum("shqk,shkd->shqd", weights_half, values, preferred_element_type=jnp.float32)
    )
    attended = lax.all_gather(from_heads(attended_heads), "seq", axis=0, tiled=False)
    attended = jnp.transpose(attended, (1, 0, 2)).reshape(all_rows, model_width)
    projected = lax.all_to_all(
        halved(jnp.dot(attended, out_part, preferred_element_type=jnp.float32)).reshape(
            slot_count, length, part_width
        ),
        "seq",
        1,
        2,
        tiled=True,
    ).reshape(row_count, model_width)
    middle = flat_tokens + projected + vec_one[4]
    normed_two, inverse_two = normalize(middle)
    lifted_two = gather_rows(halved(normed_two * vec_two[0] + vec_two[1]))
    upper = jnp.dot(lifted_two, up_part, preferred_element_type=jnp.float32) + bias_part
    active_full, slope = gelu_pair(upper)
    active = halved(active_full)
    upper_grad = (
        lax.dot_general(
            cot_all, down_part, (((1,), (1,)), ((), ())), preferred_element_type=jnp.float32
        )
        * slope
    )
    upper_half = halved(upper_grad)
    lift_two_grad = scatter_rows(
        lax.dot_general(
            upper_half, up_part, (((1,), (1,)), ((), ())), preferred_element_type=jnp.float32
        )
    )
    fed = scatter_rows(jnp.dot(active, down_part, preferred_element_type=jnp.float32))
    block_output = (middle + fed + vec_two[2]).reshape(
        slot_count, block_size, model_width
    ) * live_mask

    def outer(left, right):
        return halved(
            lax.dot_general(
                left, right, (((0,), (0,)), ((), ())), preferred_element_type=jnp.float32
            )
        )

    shrink_sum = lax.psum_scatter(
        outer(active, cot_all), "dp", scatter_dimension=0, tiled=True
    ).astype(jnp.float32)
    expand_sum = collect_columns(
        lax.psum_scatter(outer(lifted_two, upper_half), "dp", scatter_dimension=0, tiled=True),
        groups,
        hidden_part,
    ).astype(jnp.float32)
    bias_grad = jnp.sum(upper_grad, axis=0).reshape(replicas, 1, hidden_part)

    gain_two_grad = jnp.sum(lift_two_grad * normed_two, axis=0)
    shift_two_grad = jnp.sum(lift_two_grad, axis=0)
    middle_grad = cotangent + norm_back(lift_two_grad * vec_two[0], normed_two, inverse_two)
    middle_half = halved(middle_grad)
    out_bias_grad = jnp.sum(middle_grad, axis=0)
    middle_cols = lax.all_to_all(
        middle_half.reshape(slot_count, block_size, model_width), "seq", 2, 1, tiled=True
    ).reshape(all_rows, part_width)
    attended_back = halved(
        lax.dot_general(
            middle_cols, out_part, (((1,), (1,)), ((), ())), preferred_element_type=jnp.float32
        )
    )
    attended_grad = to_heads(
        lax.psum_scatter(
            jnp.transpose(attended_back.reshape(all_rows, groups, part_width), (1, 0, 2)),
            "seq",
            scatter_dimension=0,
            tiled=True,
        ).reshape(all_rows, part_width)
    )
    outward_part = outer(attended, middle_cols)
    delta_sum = jnp.sum(
        attended_grad.astype(jnp.float32) * attended_heads.astype(jnp.float32),
        axis=-1,
        keepdims=True,
    )
    weight_grad = jnp.einsum(
        "shqd,shkd->shqk", attended_grad, values, preferred_element_type=jnp.float32
    )
    score_grad = halved(weights_full * (weight_grad - delta_sum) * score_scale)
    query_grad = from_heads(
        jnp.einsum("shqk,shkd->shqd", score_grad, keys, preferred_element_type=jnp.float32)
    )
    key_grad = from_heads(
        jnp.einsum("shqk,shqd->shkd", score_grad, queries, preferred_element_type=jnp.float32)
    )
    value_grad = from_heads(
        jnp.einsum(
            "shqk,shqd->shkd", weights_half, attended_grad, preferred_element_type=jnp.float32
        )
    )
    packed_grad = halved(jnp.concatenate([query_grad, key_grad, value_grad], axis=1))
    lift_one_grad = scatter_rows(
        lax.dot_general(
            packed_grad, in_part, (((1,), (1,)), ((), ())), preferred_element_type=jnp.float32
        )
    )
    inward_part = outer(lifted_one, packed_grad)

    def place_part(part):
        return lax.dynamic_update_slice_in_dim(
            jnp.zeros((model_width,), jnp.float32), part, mine * part_width, 0
        )

    gain_one_grad = jnp.sum(lift_one_grad * normed_one, axis=0)
    shift_one_grad = jnp.sum(lift_one_grad, axis=0)
    tokens_grad = middle_grad + norm_back(lift_one_grad * vec_one[0], normed_one, inverse_one)
    input_gradient = tokens_grad.reshape(slot_count, block_size, model_width) * live_mask
    vector_grads = jnp.stack(
        [
            gain_one_grad,
            shift_one_grad,
            place_part(jnp.sum(query_grad, axis=0)),
            place_part(jnp.sum(value_grad, axis=0)),
            out_bias_grad,
            gain_two_grad,
            shift_two_grad,
            feed_bias_grad,
        ]
    ).reshape(8, devices, vec_width)
    bias_placed = lax.dynamic_update_slice_in_dim(
        jnp.zeros((replicas, groups, hidden_part), jnp.float32), bias_grad, mine, 1
    ).reshape(devices, hidden_part)
    small_grads = halved(
        jnp.concatenate(
            [jnp.transpose(vector_grads, (1, 0, 2)).reshape(devices, 8 * vec_width), bias_placed],
            axis=1,
        )
    ).reshape(replicas, groups, small_size)
    small_grads = jnp.pad(
        small_grads, ((0, 0), (0, pad_rows - groups), (0, model_width - small_size))
    )
    both_grads = jnp.concatenate([inward_part, outward_part], axis=1).reshape(
        replicas, block_rows, model_width
    )
    reduced = lax.psum_scatter(
        jnp.concatenate([both_grads, small_grads], axis=1).reshape(-1, model_width),
        "dp",
        scatter_dimension=0,
        tiled=True,
    )
    returned = lax.all_to_all(
        jnp.concatenate(
            [
                reduced[:block_rows].reshape(groups, in_rows, model_width),
                reduced[block_rows : block_rows + groups].reshape(groups, 1, model_width),
            ],
            axis=1,
        ),
        "seq",
        0,
        0,
        tiled=True,
    )
    both_sum = jnp.transpose(
        returned[:, :in_rows].reshape(groups, in_rows, -1, part_width), (1, 2, 0, 3)
    ).reshape(in_rows, -1).astype(jnp.float32)
    inward_sum = both_sum[:, : 3 * model_width]
    outward_sum = both_sum[:, 3 * model_width :]
    small_sum = jnp.sum(returned[:, in_rows, :small_size].astype(jnp.float32), axis=0)
    vector_sum = small_sum[: 8 * vec_width].reshape(8, vec_width)
    attend_vec_sum = vector_sum[:5]
    feed_vec_sum = vector_sum[5:]
    bias_sum = small_sum[8 * vec_width :]
    inward_new, inward_state = adamw_update(inward, inward_sum, inward_moments, weight_decay)
    outward_new, outward_state = adamw_update(outward, outward_sum, outward_moments, weight_decay)
    attend_new, attend_state = adamw_update(attend_vectors, attend_vec_sum, attend_moments, 0.0)
    expand_new, expand_state = adamw_update(expand, expand_sum, expand_moments, weight_decay)
    shrink_new, shrink_state = adamw_update(shrink, shrink_sum, shrink_moments, weight_decay)
    feed_new, feed_state = adamw_update(feed_vectors, feed_vec_sum, feed_moments, 0.0)
    bias_new, bias_state = adamw_update(expand_bias, bias_sum, bias_moments, 0.0)
    return (
        block_output,
        input_gradient,
        inward_sum,
        outward_sum,
        attend_vec_sum,
        expand_sum,
        shrink_sum,
        feed_vec_sum,
        bias_sum,
        inward_new,
        outward_new,
        attend_new,
        expand_new,
        shrink_new,
        feed_new,
        bias_new,
        inward_state,
        outward_state,
        attend_state,
        expand_state,
        shrink_state,
        feed_state,
        bias_state,
    )


MESH = pl.DeviceIdType.MESH
copy_slots = 160


def mm(left, right):
    return lax.dot_general(
        left, right, (((1,), (0,)), ((), ())), preferred_element_type=jnp.float32
    )


def mm_nt(left, right):
    return lax.dot_general(
        left, right, (((1,), (1,)), ((), ())), preferred_element_type=jnp.float32
    )


def mm_tn(left, right):
    return lax.dot_general(
        left, right, (((0,), (0,)), ((), ())), preferred_element_type=jnp.float32
    )


def wide(operand):
    return operand.astype(jnp.float32)


def scratch_plan(slots, length, block, width, head_count, in_rows, hidden):
    half, full = jnp.bfloat16, jnp.float32
    rows = slots * block
    part = head_count * HEAD_DIM
    dp_rows = in_rows * 4
    pairs = slots * head_count
    return dict(
        tokens=((rows, width), full),
        cot=((rows, width), full),
        inward=((in_rows, 3 * width), full),
        outward=((in_rows, width), full),
        expand=((in_rows, 4 * hidden), full),
        shrink=((hidden // 8, width), full),
        s_in=((4, in_rows, 3 * part), half),
        s_up=((4, in_rows, hidden), half),
        in_all=((width, 4 * part), half),
        up_all=((width, hidden), half),
        down_all=((hidden, width), half),
        out_ring=((4, 2, in_rows, width), half),
        out_all=((4, 2, in_rows, width), half),
        live=((rows, 1), full),
        small=((16, 128), full),
        small_land=((4, 8, 128), full),
        small_all=((8, 16, 128), full),
        vecs=((16, width), full),
        normed_one=((rows, width), full),
        inverse_one=((rows, 1), full),
        lifted_one=((slots, length, width), half),
        cot_all=((slots, length, width), half),
        q_h=((pairs, length, HEAD_DIM), half),
        k_h=((pairs, length, HEAD_DIM), half),
        v_h=((pairs, length, HEAD_DIM), half),
        weights=((pairs, length, length), full),
        att_h=((pairs, length, HEAD_DIM), half),
        attended=((slots, length, part), half),
        proj_p=((slots, length, width), half),
        proj_c=((2, slots, block, width), half),
        proj_b=((slots, block, width), half),
        proj_y=((slots, block, width), half),
        middle=((rows, width), full),
        normed_two=((rows, width), full),
        inverse_two=((rows, 1), full),
        lifted_two=((slots, length, width), half),
        active=((slots, length, hidden), half),
        slope=((slots, length, hidden), full),
        upper_half=((slots, length, hidden), half),
        two_p=((slots, length, width), half),
        two_c=((2, slots, block, width), half),
        two_b=((slots, block, width), half),
        two_y=((slots, block, width), half),
        fed_p=((slots, length, width), half),
        fed_c=((2, slots, block, width), half),
        fed_b=((slots, block, width), half),
        fed_y=((slots, block, width), half),
        one_p=((slots, length, width), half),
        one_c=((2, slots, block, width), half),
        one_b=((slots, block, width), half),
        one_y=((slots, block, width), half),
        mid_all=((slots, length, width), half),
        mid_grad=((rows, width), full),
        ag_h=((pairs, length, HEAD_DIM), half),
        pg_h=((3, pairs, length, HEAD_DIM), half),
        bias_h=((2, pairs, 1, HEAD_DIM), full),
        pg=((slots, length, 3 * part), half),
        sh_s=((2, 4, dp_rows, width), half),
        sh_l=((2, 4, dp_rows, width), half),
        ex_s=((2, 4, dp_rows, hidden), half),
        ex_l=((2, 4, dp_rows, hidden), half),
        ex_f=((dp_rows, hidden), half),
        ex_g=((4, in_rows, hidden), half),
        low_s=((2, 4, dp_rows, 2 * part), half),
        low_l=((2, 4, dp_rows, 2 * part), half),
        high_s=((2, 4, dp_rows, 2 * part), half),
        high_l=((2, 4, dp_rows, 2 * part), half),
        in_f=((dp_rows, 3 * part), half),
        in_g=((4, in_rows, 3 * part), half),
        og=((4, 2, in_rows, width), half),
        og_ring=((4, 2, in_rows, width), half),
        g_full=((16, width), full),
        g_out=((2, 4, 16, 128), full),
        g_l=((4, 16, 128), full),
        g_z=((3, 16, 128), full),
        g_f=((8, 128), full),
        g_g=((4, 8, 128), full),
    )


def layer_kernel(names, *refs):
    r = types.SimpleNamespace(**dict(zip(names, refs)))
    ssem, rsem = r.ssem, r.rsem
    slots, length, width = r.lifted_one.shape
    rows = r.middle.shape[0]
    block = rows // slots
    pairs = r.q_h.shape[0]
    heads = pairs // slots
    part = heads * HEAD_DIM
    in_rows = r.outward.shape[0]
    dp_rows = 4 * in_rows
    hidden = r.up_all.shape[1]
    score_scale = 1.0 / math.sqrt(HEAD_DIM)

    dp, me = lax.axis_index("dp"), lax.axis_index("seq")
    z, x = dp // 2, dp % 2
    y, core = me // 2, me % 2
    sib = me + 1 - 2 * core
    yp = (me + 2) % 4
    xdp = dp + 1 - 2 * x
    turn = y + 2 * core

    def z_dp(k):
        return 2 * ((z + k) % 4) + x

    place = (1 - x) * z + x * (7 - z)

    def ring_dp(k):
        at = (place + k + 8) % 8
        return (1 - at // 4) * 2 * at + (at // 4) * (15 - 2 * at)

    right, left = (ring_dp(1), me), (ring_dp(-1), me)

    used = [0]
    sent = []

    def slot():
        used[0] += 1
        return used[0] - 1

    def rc(source, target, device, at=None, start=True):
        index = slot() if at is None else at
        copy = pltpu.make_async_remote_copy(
            source,
            target,
            ssem.at[index],
            rsem.at[index],
            device_id=device,
            device_id_type=MESH,
        )
        if start:
            copy.start()
            if at is None:
                sent.append(copy)
        return copy

    loads = [
        pltpu.make_async_copy(source, target, r.load_sem.at[index])
        for index, (source, target) in enumerate(
            (
                (r.shrink_far, r.shrink),
                (r.inward_far, r.inward),
                (r.outward_far, r.outward),
                (r.expand_far, r.expand),
                (r.tokens_far, r.tokens),
                (r.cot_far, r.cot),
            )
        )
    ]
    for load in loads:
        load.start()
    barrier = pltpu.get_barrier_semaphore()
    for device in (
        [(dp, (me + k) % 4) for k in (1, 2, 3)]
        + [(z_dp(k), me) for k in (1, 2, 3)]
        + [(xdp, me)]
    ):
        pl.semaphore_signal(barrier, inc=1, device_id=device, device_id_type=MESH)

    def seq_rows(which):
        return pl.ds(which * block, block)

    class SeqGather:
        def __init__(self, buf):
            self.buf = buf
            own = seq_rows(me)
            self.far = [rc(buf.at[s, own], buf.at[s, own], (dp, yp)) for s in range(slots)]
            self.near = rc(buf.at[:, own], buf.at[:, own], (dp, sib))

        def forward(self):
            theirs = seq_rows(yp)
            self.passed = []
            for s in range(slots):
                self.far[s].wait_recv()
                self.passed.append(
                    rc(self.buf.at[s, theirs], self.buf.at[s, theirs], (dp, sib))
                )

        def finish(self):
            self.near.wait_recv()
            for copy in self.passed:
                copy.wait_recv()

    class SeqScatter:
        def __init__(self, partial, near, sums, far):
            self.p, self.c, self.b, self.y = partial, near, sums, far
            self.base = slot()
            slot()

        def near_copy(self, index, which):
            return rc(
                self.p.at[:, seq_rows(which)],
                self.c.at[1 - index],
                (dp, sib),
                at=self.base + index,
                start=False,
            )

        def order(self, index):
            return (me + (1 - index // 2) * (sib - me) + 2 * (1 - index % 2)) % 4

        def fill(self, compute):
            def step(index, carry):
                which = self.order(index)
                value = compute(which)
                self.p[:, seq_rows(which)] = halved(value).reshape(slots, block, width)

                @pl.when(index < 2)
                def _():
                    self.near_copy(index, which).start()

                return carry

            lax.fori_loop(0, 4, step, 0)
            for index in range(2):
                sent.append(self.near_copy(index, self.order(index)))

        def middle(self):
            self.near_copy(0, self.order(0)).wait_recv()
            self.far = []
            for s in range(slots):
                self.b[s] = halved(wide(self.p[s, seq_rows(yp)]) + wide(self.c[1, s]))
                self.far.append(rc(self.b.at[s], self.y.at[s], (dp, yp)))

        def finish(self):
            self.near_copy(1, self.order(1)).wait_recv()
            for copy in self.far:
                copy.wait_recv()
            total = wide(self.p[:, seq_rows(me)]) + wide(self.c[0]) + wide(self.y[...])
            return total.reshape(rows, width)

    class SmallGather:
        def __init__(self, buf):
            self.buf = buf

        def send(self):
            own = self.buf.at[dp]
            self.far = [rc(own, own, (z_dp(k), me)) for k in (1, 2, 3)]
            self.near = [rc(own, own, (xdp, me))]

        def forward(self):
            for k in (1, 2, 3):
                self.far[k - 1].wait_recv()
                theirs = self.buf.at[z_dp(4 - k)]
                self.near.append(rc(theirs, theirs, (xdp, me)))

        def finish(self):
            for copy in self.near:
                copy.wait_recv()

    half_rows = dp_rows // 2

    class RingGather:
        def __init__(self, buf):
            self.buf, self.moving = buf, []

        def at(self, which, piece=None):
            start = which * dp_rows
            if piece is None:
                return self.buf.at[pl.ds(pl.multiple_of(start, dp_rows), dp_rows)]
            start = start + piece * half_rows
            return self.buf.at[pl.ds(pl.multiple_of(start, half_rows), half_rows)]

        def step(self, j):
            self.finish()
            ahead = self.at(ring_dp(1 - j), 0 if j == 4 else None)
            back = self.at(ring_dp(j - 1), 1 if j == 4 else None)
            self.moving = [rc(ahead, ahead, right), rc(back, back, left)]

        def finish(self):
            for copy in self.moving:
                copy.wait_recv()

    class RingScatter:
        def __init__(self, chunk, away, land):
            self.chunk, self.away, self.land, self.moving = chunk, away, land, []

        def arrive(self):
            for copy in self.moving:
                copy.wait_recv()

        def step(self, j):
            if j == 1:
                value = halved(self.chunk(ring_dp(4)))
                here = slice(0, half_rows)
                self.away[0, 0, here] = value[:half_rows]
                self.away[1, 0, here] = value[half_rows:]
                rows_sent = pl.ds(0, half_rows)
            else:
                ahead, back = self.chunk(ring_dp(5 - j)), self.chunk(ring_dp(j - 5))
                self.arrive()
                if j == 2:
                    near = wide(self.land[0, 0, 0:half_rows])
                    far = wide(self.land[1, 0, 0:half_rows])
                    self.away[0, 1, 0:half_rows] = halved(ahead[:half_rows] + near)
                    self.away[0, 1, half_rows:dp_rows] = halved(ahead[half_rows:])
                    self.away[1, 1, 0:half_rows] = halved(back[:half_rows])
                    self.away[1, 1, half_rows:dp_rows] = halved(back[half_rows:] + far)
                else:
                    self.away[0, j - 1] = halved(ahead + wide(self.land[0, j - 2]))
                    self.away[1, j - 1] = halved(back + wide(self.land[1, j - 2]))
                rows_sent = pl.ds(0, dp_rows)
            self.moving = [
                rc(
                    self.away.at[way, j - 1, rows_sent],
                    self.land.at[way, j - 1, rows_sent],
                    target,
                )
                for way, target in ((0, right), (1, left))
            ]

        def finish(self):
            own = self.chunk(dp)
            self.arrive()
            return own + (wide(self.land[0, 3]) + wide(self.land[1, 3]))

    def chunk_of(left_ref, right_ref):
        def chunk(which):
            at = pl.ds(pl.multiple_of(which * dp_rows, dp_rows), dp_rows)
            return mm_tn(
                left_ref[:, :, at].reshape(-1, dp_rows), right_ref[...].reshape(slots * length, -1)
            )

        return chunk

    vec_width = r.attend_vectors.shape[1]
    r.small[0:5, 0:vec_width] = r.attend_vectors[...]
    r.small[5:8, 0:vec_width] = r.feed_vectors[...]
    spread = jnp.concatenate([r.small[0:8, 0:vec_width]] * 4, axis=1)
    lane = lax.broadcasted_iota(jnp.int32, spread.shape, 1)
    r.small[0:8] = wide(halved(jnp.where(lane // vec_width == me, spread, 0.0)))
    r.small[8:16] = jnp.broadcast_to(wide(halved(r.expand_bias[...])), (8, 128))
    for s in range(slots):
        found = jnp.int32(0)
        for i in range(r.placement.shape[0]):
            found = jnp.where(r.placement[i] == dp * slots + s, 1, found)
        r.live[s * block : (s + 1) * block] = jnp.full((block, 1), found.astype(jnp.float32))

    dp_at = pl.ds(pl.multiple_of(dp * dp_rows, dp_rows), dp_rows)
    own_at = pl.ds(pl.multiple_of(dp * dp_rows + me * in_rows, in_rows), in_rows)
    loads[0].wait()
    r.down_all[dp_at] = halved(r.shrink[...])
    r.small_land[0] = r.small[0:8]
    down, inward, up = RingGather(r.down_all), RingGather(r.in_all), RingGather(r.up_all)
    pl.semaphore_wait(barrier, 7)
    down.step(1)
    small_seq = [
        rc(r.small_land.at[0], r.small_land.at[k], (dp, (me + k) % 4)) for k in (1, 2, 3)
    ]

    loads[1].wait()
    for g in range(4):
        turn_g = g // 2 + 2 * (g % 2)
        for third in range(3):
            pieces = [
                r.inward[:, pl.ds(third * width + (4 * j + turn_g) * HEAD_DIM, HEAD_DIM)]
                for j in range(heads)
            ]
            r.s_in[g, :, third * part : (third + 1) * part] = halved(
                jnp.concatenate(pieces, axis=1)
            )
    in_at = r.in_all.at[own_at, pl.ds(0, 3 * part)]
    in_seq = [
        rc(r.s_in.at[(me + k) % 4], in_at, (dp, (me + k) % 4)) for k in (2, 3, 1)
    ]
    in_at[...] = r.s_in[me]
    loads[2].wait()
    for i in range(4):
        rows_at = pl.ds(pl.multiple_of(dp * dp_rows + i * in_rows, in_rows), in_rows)
        r.in_all[rows_at, 3 * part : 4 * part] = halved(r.outward[:, i * part : (i + 1) * part])
    loads[3].wait()
    for g in range(4):
        for d in range(hidden // 128):
            r.s_up[g, :, d * 128 : (d + 1) * 128] = halved(
                r.expand[:, pl.ds((d * 4 + g) * 128, 128)]
            )
    up_seq = [
        rc(r.s_up.at[(me + k) % 4], r.up_all.at[own_at], (dp, (me + k) % 4))
        for k in (2, 3, 1)
    ]
    r.up_all[own_at] = r.s_up[me]

    loads[4].wait()
    loads[5].wait()
    normed, inverse = normalize(r.tokens[...])
    r.normed_one[...] = normed
    r.inverse_one[...] = inverse
    cotangent = r.cot[...] * r.live[...]
    r.cot_all[:, seq_rows(me)] = halved(cotangent).reshape(slots, block, width)

    for copy in small_seq:
        copy.wait_recv()
    mine_small = r.small_all.at[dp]
    mine_small[0:8] = (r.small_land[0] + r.small_land[1]) + (
        r.small_land[2] + r.small_land[3]
    )
    mine_small[8:16] = r.small[8:16]
    small = SmallGather(r.small_all)
    small.send()

    for copy in in_seq:
        copy.wait_recv()
    inward.step(1)
    small.forward()
    inward.step(2)
    down.step(2)
    small.finish()
    for d in range(8):
        r.vecs[:, d * 128 : (d + 1) * 128] = r.small_all[d]

    def vec(index):
        return r.vecs[index : index + 1, :]

    r.lifted_one[:, seq_rows(me)] = halved(
        r.normed_one[...] * vec(0) + vec(1)
    ).reshape(slots, block, width)
    lift_one = SeqGather(r.lifted_one)

    inward.step(3)
    down.step(3)
    lift_one.forward()
    cot = SeqGather(r.cot_all)
    inward.step(4)
    for copy in up_seq:
        copy.wait_recv()
    up.step(1)
    cot.forward()
    down.step(4)
    lift_one.finish()
    inward.finish()
    up.step(2)
    for d in range(8):
        r.out_ring[d // 2, d % 2] = jnp.concatenate(
            [
                r.in_all[d * dp_rows + i * in_rows : d * dp_rows + (i + 1) * in_rows, 3 * part :]
                for i in range(4)
            ],
            axis=1,
        )
    r.out_all[:, core] = r.out_ring[:, core]
    out_pair = rc(r.out_ring.at[:, 1 - core], r.out_all.at[:, core], (dp, sib))

    def own_heads(row):
        pieces = []
        for j in range(heads):
            piece = jnp.zeros((1, HEAD_DIM), jnp.float32)
            for t in range(4):
                start = (4 * j + t) * HEAD_DIM
                piece = jnp.where(turn == t, row[:, start : start + HEAD_DIM], piece)
            pieces.append(piece)
        return jnp.concatenate(pieces, axis=1)

    bias_query, bias_value = own_heads(vec(2)), own_heads(vec(3))

    def project_in(s, carry):
        packed = mm(r.lifted_one[s], r.in_all[:, : 3 * part])
        queries = halved(packed[:, :part] + bias_query)
        keys = halved(packed[:, part : 2 * part])
        values = halved(packed[:, 2 * part :] + bias_value)
        for j in range(heads):
            cut = slice(j * HEAD_DIM, (j + 1) * HEAD_DIM)
            r.q_h[s * heads + j] = queries[:, cut]
            r.k_h[s * heads + j] = keys[:, cut]
            r.v_h[s * heads + j] = values[:, cut]
        return carry

    lax.fori_loop(0, slots, project_in, 0)

    def attend(p, carry):
        scores = mm_nt(r.q_h[p], r.k_h[p]) * score_scale
        row_at = lax.broadcasted_iota(jnp.int32, scores.shape, 0)
        column_at = lax.broadcasted_iota(jnp.int32, scores.shape, 1)
        scores = jnp.where(column_at <= row_at, scores, masked_score)
        peak = jnp.max(scores, axis=-1, keepdims=True)
        raised = jnp.exp(scores - peak)
        weights = raised * (1.0 / jnp.sum(raised, axis=-1, keepdims=True))
        r.weights[p] = weights
        r.att_h[p] = halved(mm(halved(weights), r.v_h[p]))
        return carry

    lax.fori_loop(0, pairs, attend, 0)
    for s in range(slots):
        r.attended[s] = jnp.concatenate(
            [r.att_h[s * heads + j] for j in range(heads)], axis=1
        )

    up.step(3)
    out_pair.wait_recv()
    proj = SeqScatter(r.proj_p, r.proj_c, r.proj_b, r.proj_y)
    proj.fill(
        lambda which: mm(
            r.attended[:, seq_rows(which)].reshape(rows, part), r.out_all[...].reshape(part, width)
        )
    )
    proj.middle()
    up.step(4)
    middle = r.tokens[...] + proj.finish() + vec(4)
    r.middle[...] = middle
    normed, inverse = normalize(middle)
    r.normed_two[...] = normed
    r.inverse_two[...] = inverse
    r.lifted_two[:, seq_rows(me)] = halved(normed * vec(5) + vec(6)).reshape(
        slots, block, width
    )
    lift_two = SeqGather(r.lifted_two)
    lift_two.forward()
    lift_two.finish()
    cot.finish()
    up.finish()

    def feed(index, carry):
        here = seq_rows(index)
        upper = mm(r.lifted_two[:, here].reshape(rows, width), r.up_all[...]) + vec(8)
        active, slope = gelu_pair(upper)
        r.active[:, here] = halved(active).reshape(slots, block, hidden)
        r.slope[:, here] = slope.reshape(slots, block, hidden)
        return carry

    lax.fori_loop(0, 4, feed, 0)
    shrink = RingScatter(chunk_of(r.active, r.cot_all), r.sh_s, r.sh_l)
    shrink.step(1)
    down.finish()

    two = SeqScatter(r.two_p, r.two_c, r.two_b, r.two_y)
    r.g_full[8:9, :] = jnp.zeros((1, hidden), jnp.float32)

    def feed_back(which):
        here = seq_rows(which)
        upper_grad = mm_nt(
            r.cot_all[:, here].reshape(rows, width), r.down_all[...]
        ) * r.slope[:, here].reshape(rows, hidden)
        r.g_full[8:9, :] += jnp.sum(upper_grad, axis=0, keepdims=True)
        upper_half = halved(upper_grad)
        r.upper_half[:, here] = upper_half.reshape(slots, block, hidden)
        return mm_nt(upper_half, r.up_all[...])

    two.fill(feed_back)
    two.middle()
    expand = RingScatter(chunk_of(r.lifted_two, r.upper_half), r.ex_s, r.ex_l)
    expand.step(1)
    shrink.step(2)
    fed = SeqScatter(r.fed_p, r.fed_c, r.fed_b, r.fed_y)
    fed.fill(
        lambda which: mm(r.active[:, seq_rows(which)].reshape(rows, hidden), r.down_all[...])
    )
    expand.step(2)
    lift_grad = two.finish()
    normed = r.normed_two[...]
    r.g_full[5:6, :] = jnp.sum(lift_grad * normed, axis=0, keepdims=True)
    r.g_full[6:7, :] = jnp.sum(lift_grad, axis=0, keepdims=True)
    cotangent = r.cot[...] * r.live[...]
    r.g_full[7:8, :] = jnp.sum(cotangent, axis=0, keepdims=True)
    middle_grad = cotangent + norm_back(lift_grad * vec(5), normed, r.inverse_two[...])
    r.mid_grad[...] = middle_grad
    r.g_full[4:5, :] = jnp.sum(middle_grad, axis=0, keepdims=True)
    r.mid_all[:, seq_rows(me)] = halved(middle_grad).reshape(slots, block, width)
    mid = SeqGather(r.mid_all)
    shrink.step(3)
    mid.forward()
    fed.middle()
    expand.step(3)
    mid.finish()

    for s in range(slots):
        grads = halved(mm_nt(r.mid_all[s], r.out_all[...].reshape(part, width)))
        for j in range(heads):
            r.ag_h[s * heads + j] = grads[:, j * HEAD_DIM : (j + 1) * HEAD_DIM]

    r.og[...] = halved(
        mm_tn(
            r.attended[...].reshape(slots * length, part),
            r.mid_all[...].reshape(slots * length, width),
        )
    ).reshape(4, 2, in_rows, width)
    r.og_ring[:, core] = r.og[:, core]
    og_pair = rc(r.og.at[:, 1 - core], r.og_ring.at[:, core], (dp, sib))
    shrink.step(4)

    def attend_back(p, carry):
        weights, grads = r.weights[p], r.ag_h[p]
        delta = jnp.sum(wide(grads) * wide(r.att_h[p]), axis=-1, keepdims=True)
        weight_grad = mm_nt(grads, r.v_h[p])
        score_grad = halved(weights * (weight_grad - delta) * score_scale)
        query_grad = mm(score_grad, r.k_h[p])
        key_grad = mm_tn(score_grad, r.q_h[p])
        value_grad = mm_tn(halved(weights), grads)
        r.bias_h[0, p] = jnp.sum(query_grad, axis=0, keepdims=True)
        r.bias_h[1, p] = jnp.sum(value_grad, axis=0, keepdims=True)
        r.pg_h[0, p] = halved(query_grad)
        r.pg_h[1, p] = halved(key_grad)
        r.pg_h[2, p] = halved(value_grad)
        return carry

    lax.fori_loop(0, pairs, attend_back, 0)
    for s in range(slots):
        r.pg[s] = jnp.concatenate(
            [r.pg_h[i, s * heads + j] for i in range(3) for j in range(heads)], axis=1
        )
    expand.step(4)
    og_pair.wait_recv()

    half_width = 2 * part

    def low_chunk(which):
        return chunk_of(r.lifted_one, r.pg.at[:, :, 0:half_width])(which)

    def high_chunk(which):
        ours = r.og_ring[which // 2, which % 2]
        packed = jnp.concatenate(
            [ours[:, i * part : (i + 1) * part] for i in range(4)], axis=0
        )
        last = chunk_of(r.lifted_one, r.pg.at[:, :, half_width : 3 * part])(which)
        return jnp.concatenate([last, wide(packed)], axis=1)

    low = RingScatter(low_chunk, r.low_s, r.low_l)
    high = RingScatter(high_chunk, r.high_s, r.high_l)
    low.step(1)
    high.step(1)
    one = SeqScatter(r.one_p, r.one_c, r.one_b, r.one_y)
    one.fill(
        lambda which: mm_nt(
            r.pg[:, seq_rows(which)].reshape(rows, 3 * part), r.in_all[:, : 3 * part]
        )
    )
    one.middle()
    low.step(2)
    high.step(2)

    block_output = r.middle[...] + fed.finish() + vec(7)
    r.block_output[...] = block_output * r.live[...]
    r.shrink_sum[...] = shrink.finish()
    lift_grad = one.finish()
    normed = r.normed_one[...]
    r.g_full[0:1, :] = jnp.sum(lift_grad * normed, axis=0, keepdims=True)
    r.g_full[1:2, :] = jnp.sum(lift_grad, axis=0, keepdims=True)
    input_gradient = r.mid_grad[...] + norm_back(
        lift_grad * vec(0), normed, r.inverse_one[...]
    )
    r.input_gradient[...] = input_gradient * r.live[...]
    for i in range(2):
        pieces = []
        for head in range(4 * heads):
            total = jnp.zeros((1, HEAD_DIM), jnp.float32)
            for s in range(slots):
                total = total + r.bias_h[i, s * heads + head // 4]
            pieces.append(jnp.where(turn == head % 4, total, 0.0))
        r.g_full[2 + i : 3 + i, :] = jnp.concatenate(pieces, axis=1)
    r.g_full[9:16, :] = jnp.zeros((7, width), jnp.float32)
    for d in range(8):
        r.g_out[d % 2, d // 2] = r.g_full[:, d * 128 : (d + 1) * 128]
    g_near = rc(r.g_out.at[1 - x], r.g_l, (xdp, me))

    low.step(3)
    high.step(3)
    g_near.wait_recv()
    r.g_l[...] = r.g_l[...] + r.g_out[x]
    g_far = [rc(r.g_l.at[(z + k) % 4], r.g_z.at[k - 1], (z_dp(k), me)) for k in (1, 2, 3)]

    r.ex_f[...] = halved(expand.finish())

    def sub(buf, which):
        return buf.at[pl.ds(pl.multiple_of(which * in_rows, in_rows), in_rows)]

    def seq_return(buf, land):
        land[0] = buf[pl.ds(pl.multiple_of(me * in_rows, in_rows), in_rows)]
        return [
            rc(sub(buf, (me + k) % 4), land.at[k], (dp, (me + k) % 4)) for k in (2, 3, 1)
        ]

    ex_back = seq_return(r.ex_f, r.ex_g)
    low.step(4)
    high.step(4)
    for copy in g_far:
        copy.wait_recv()
    g_total = r.g_l[z] + r.g_z[0] + r.g_z[1] + r.g_z[2]
    r.g_f[...] = g_total[0:8]
    r.g_g[0] = g_total[0:8]
    g_back = [rc(r.g_f, r.g_g.at[k], (dp, (me + k) % 4)) for k in (1, 2, 3)]

    for copy in ex_back:
        copy.wait_recv()
    for k in range(4):
        for g in range(4):

            @pl.when((me - k + 4) % 4 == g)
            def _():
                value = wide(r.ex_g[k])
                for d in range(hidden // 128):
                    start = (d * 4 + g) * 128
                    r.expand_sum[:, start : start + 128] = value[:, d * 128 : (d + 1) * 128]

    r.in_f[:, :half_width] = halved(low.finish())
    high_sum = high.finish()
    r.in_f[:, half_width:] = halved(high_sum[:, :part])
    for i in range(4):
        r.outward_sum[:, i * part : (i + 1) * part] = high_sum[
            i * in_rows : (i + 1) * in_rows, part:
        ]
    in_back = seq_return(r.in_f, r.in_g)
    for copy in g_back:
        copy.wait_recv()
    vector_total = (r.g_g[0] + r.g_g[1]) + (r.g_g[2] + r.g_g[3])
    vector_own = jnp.zeros((8, vec_width), jnp.float32)
    for g in range(4):
        vector_own = jnp.where(
            me == g, vector_total[:, g * vec_width : (g + 1) * vec_width], vector_own
        )
    r.attend_sum[...] = vector_own[0:5]
    r.feed_sum[...] = vector_own[5:8]
    r.bias_sum[...] = g_total[8:9]
    for copy in in_back:
        copy.wait_recv()
    by_seq = []
    for g in range(4):
        by_seq.append(r.in_g[(me - g + 4) % 4])
    for third in range(3):
        pieces = []
        for head in range(4 * heads):
            g = 2 * (head % 2) + (head // 2) % 2
            start = third * part + (head // 4) * HEAD_DIM
            pieces.append(by_seq[g][:, start : start + HEAD_DIM])
        r.inward_sum[:, third * width : (third + 1) * width] = wide(
            jnp.concatenate(pieces, axis=1)
        )

    for copy in sent:
        copy.wait_send()


def adamw_kernel(decays, count, *refs):
    kinds = len(decays)
    masters, sums, moments = refs[:kinds], refs[kinds : 2 * kinds], refs[2 * kinds : 3 * kinds]
    passed = refs[3 * kinds : 3 * kinds + count]
    outs = refs[3 * kinds + count :]
    for i, decay in enumerate(decays):
        gradient = sums[i][...]
        fresh, state = outs[kinds + i], outs[2 * kinds + i]
        parameter = masters[i][...]
        turned = moments[i].shape[0] == gradient.shape[0]
        if turned:
            old_first, old_second = moments[i][:, 0], moments[i][:, 1]
        else:
            old_first, old_second = moments[i][0], moments[i][1]
        first_moment = beta_first * old_first + (1.0 - beta_first) * gradient
        second = beta_second * old_second + (1.0 - beta_second) * gradient * gradient
        unbiased_first = first_moment * (1.0 / (1.0 - beta_first**adam_steps))
        unbiased_second = second * (1.0 / (1.0 - beta_second**adam_steps))
        update = unbiased_first / (jnp.sqrt(unbiased_second) + adam_epsilon)
        fresh[...] = parameter - learn_rate * (update + decay * parameter)
        if turned:
            state[:, 0] = first_moment
            state[:, 1] = second
        else:
            state[0] = first_moment
            state[1] = second
        outs[i][...] = gradient
    for i in range(count):
        outs[3 * kinds + i][...] = passed[i][...]


def adamw_call(masters, sums, moments, decays, passed, steps):
    def spec(array):
        axis = array.ndim - 2
        small = array.shape[axis] % (8 * steps) != 0
        block = list(array.shape)
        if not small:
            block[axis] //= steps

        def index(i):
            place = [0] * array.ndim
            if not small:
                place[axis] = i
            return tuple(place)

        return pl.BlockSpec(tuple(block), index)

    arrays = [*masters, *sums, *moments, *passed]
    results = [*sums, *masters, *moments, *passed]
    return pl.pallas_call(
        functools.partial(adamw_kernel, decays, len(passed)),
        grid=(steps,),
        out_shape=[jax.ShapeDtypeStruct(array.shape, jnp.float32) for array in results],
        in_specs=[spec(array) for array in arrays],
        out_specs=[spec(array) for array in results],
        compiler_params=pltpu.CompilerParams(vmem_limit_bytes=60 * 2**20),
        name="adamw",
    )(*arrays)


def fast_body(
    tokens,
    output_cotangent,
    placement,
    inward,
    outward,
    attend_vectors,
    expand,
    shrink,
    feed_vectors,
    expand_bias,
    *moments,
):
    slot_count, block_size, model_width = tokens.shape
    groups = lax.axis_size("seq")
    row_count = slot_count * block_size
    hidden_part = expand.shape[1] // groups
    in_rows = inward.shape[0]

    plan = scratch_plan(
        slot_count,
        block_size * groups,
        block_size,
        model_width,
        HEADS // groups,
        in_rows,
        hidden_part,
    )
    inputs = dict(
        tokens_far=tokens.reshape(row_count, model_width),
        cot_far=output_cotangent.reshape(row_count, model_width),
        placement=placement,
        attend_vectors=attend_vectors,
        feed_vectors=feed_vectors,
        expand_bias=expand_bias.reshape(1, -1),
        inward_far=inward,
        outward_far=outward,
        expand_far=expand,
        shrink_far=shrink,
    )
    outputs = dict(
        block_output=(row_count, model_width),
        input_gradient=(row_count, model_width),
        inward_sum=inward.shape,
        outward_sum=outward.shape,
        expand_sum=expand.shape,
        shrink_sum=shrink.shape,
        attend_sum=attend_vectors.shape,
        feed_sum=feed_vectors.shape,
        bias_sum=(1, expand_bias.shape[0]),
    )
    names = list(inputs) + list(outputs) + list(plan) + ["ssem", "rsem", "load_sem"]
    found = pl.pallas_call(
        functools.partial(layer_kernel, names),
        out_shape=[jax.ShapeDtypeStruct(shape, jnp.float32) for shape in outputs.values()],
        in_specs=[
            pl.BlockSpec(
                memory_space=pltpu.SMEM
                if name == "placement"
                else (pl.ANY if name.endswith("_far") else pltpu.VMEM)
            )
            for name in inputs
        ],
        out_specs=[pl.BlockSpec(memory_space=pltpu.VMEM)] * len(outputs),
        scratch_shapes=[pltpu.VMEM(shape, kind) for shape, kind in plan.values()]
        + [pltpu.SemaphoreType.DMA((count,)) for count in (copy_slots, copy_slots, 6)],
        compiler_params=pltpu.CompilerParams(
            collective_id=0, has_side_effects=True, vmem_limit_bytes=60 * 2**20
        ),
        name="layer",
    )(*inputs.values())
    found = types.SimpleNamespace(**dict(zip(outputs, found)))
    sums = (
        found.inward_sum,
        found.outward_sum,
        found.attend_sum,
        found.expand_sum,
        found.shrink_sum,
        found.feed_sum,
        found.bias_sum,
    )
    masters = (
        inward,
        outward,
        attend_vectors,
        expand,
        shrink,
        feed_vectors,
        expand_bias.reshape(1, -1),
    )
    decays = (weight_decay, weight_decay, 0.0, weight_decay, weight_decay, 0.0, 0.0)

    def turned(index, moment):
        if index in (2, 5):
            return jnp.swapaxes(moment, 0, 1)
        return moment.reshape(moment.shape[:1] + masters[index].shape)

    done = list(adamw_call(
        masters,
        sums,
        [turned(index, moment) for index, moment in enumerate(moments)],
        decays,
        (found.block_output, found.input_gradient),
        2,
    ))
    kinds = len(masters)
    for index in (2, 5):
        done[2 * kinds + index] = jnp.swapaxes(done[2 * kinds + index], 0, 1)
    plain = [*masters[: kinds - 1], expand_bias]
    wanted = [*plain, *plain, *moments, tokens, tokens]
    done = [array.reshape(other.shape) for array, other in zip(done, wanted)]
    return (*done[3 * kinds :], *done[: 3 * kinds])


def solution(mesh):
    chosen = fast_body if (mesh.shape["dp"], mesh.shape["seq"]) == (8, 4) else body
    placed = (
        P("dp", "seq", None),
        P("dp", "seq", None),
        P(),
        P(("dp", "seq"), None),
        P(("dp", "seq"), None),
        P(None, ("dp", "seq")),
        P(("dp", "seq"), None),
        P(("dp", "seq"), None),
        P(None, ("dp", "seq")),
        P(("dp", "seq")),
        P(None, ("dp", "seq"), None),
        P(None, ("dp", "seq"), None),
        P(None, None, ("dp", "seq")),
        P(None, ("dp", "seq"), None),
        P(None, ("dp", "seq"), None),
        P(None, None, ("dp", "seq")),
        P(None, ("dp", "seq")),
    )
    return jax.shard_map(
        chosen,
        mesh=mesh,
        in_specs=placed,
        out_specs=(
            P("dp", "seq", None),
            P("dp", "seq", None),
            P(("dp", "seq"), None),
            P(("dp", "seq"), None),
            P(None, ("dp", "seq")),
            P(("dp", "seq"), None),
            P(("dp", "seq"), None),
            P(None, ("dp", "seq")),
            P(("dp", "seq")),
            P(("dp", "seq"), None),
            P(("dp", "seq"), None),
            P(None, ("dp", "seq")),
            P(("dp", "seq"), None),
            P(("dp", "seq"), None),
            P(None, ("dp", "seq")),
            P(("dp", "seq")),
            P(None, ("dp", "seq"), None),
            P(None, ("dp", "seq"), None),
            P(None, None, ("dp", "seq")),
            P(None, ("dp", "seq"), None),
            P(None, ("dp", "seq"), None),
            P(None, None, ("dp", "seq")),
            P(None, ("dp", "seq")),
        ),
        check_vma=False,
    )
```
